512 devices in a mesh: band: 64 (over z_lo, y, core), strip: 8 (over z_hi, x).
Axes of the slice: x: 4, y: 8, z: 8 (z_hi: 2, z_lo: 4; z = z_hi * 4 + z_lo), core: 2. Of those that a mesh axis runs over, the one named last changes fastest.
Arguments:
- activations: bfloat16 [64, 320, 48, 128], P('band', None, 'strip'), may hold values from -16 to 16
- out_grad: bfloat16 [64, 320, 48, 128], P('band', None, 'strip'), may hold values from -6 to 6
- kernel: bfloat16 [320, 9, 320], P('band', None, 'strip'), may hold values from -0.109375 to 0.109375
Outputs:
- input_grad: bfloat16 [64, 320, 48, 128], P('band', None, 'strip')
- kernel_grad: float32 [320, 9, 320], P('band', None, 'strip')
The draws below stay inside these ranges and needn't reach their ends.
All inputs are finite; a program needn't handle non-finite values.
Results may differ from the reference program's by a relative error of at most 0.001.
Values may be sent and summed in bfloat16 or wider, within the bound.
A program may use at most 64 MiB of HBM per device.

```python
import math
import jax
import jax.numpy as jnp
from jax import lax

CH = 320
TAPS = 9
WIDTH = 128
IMAGES = 64
HEIGHT = 48


def with_spikes(result, rng, source, target, blocks, factor):
    def block_of(dim):
        return (jnp.arange(result.shape[dim]) // (result.shape[dim] // blocks)).reshape((-1,) + (1,) * (result.ndim - 1 - dim))

    first = jax.random.permutation(rng, blocks)[block_of(target)]
    second = (block_of(target) + blocks // 2) % blocks
    return jnp.where((block_of(source) == first) | (block_of(source) == second), factor * result, result)


def block_scale(own_key, dims, shards, least, largest):
    def one(axis_at, parts):
        heights = jax.random.uniform(jax.random.fold_in(jax.random.fold_in(own_key, 6), axis_at), (parts,), jnp.float32, least / len(shards), largest / len(shards))
        return jnp.repeat(jnp.exp(heights), dims[axis_at] // parts).reshape((-1,) + (1,) * (len(dims) - axis_at - 1))

    loudness = one(*shards[0])
    for cut in shards[1:]:
        loudness = loudness * one(*cut)
    return loudness


def centred(own_key, shape, width, bound, split=(), held_as=jnp.bfloat16):
    factor_of = block_scale(own_key, shape, split, -0.22, 0.18) if split else 1.0
    result = jax.random.normal(own_key, shape, jnp.float32) * width * factor_of
    return jnp.minimum(jnp.maximum(result, -bound), bound).astype(held_as)


def bell_draw_with(own_key, dims, scale, reach, pieces, heavy, kind=jnp.bfloat16):
    result = scale * jax.random.normal(own_key, dims, jnp.float32)
    if pieces:
        result = result * block_scale(own_key, dims, pieces, -0.22, 0.18)
    return jnp.clip(with_spikes(result, jax.random.fold_in(own_key, 3), *heavy), -reach, reach).astype(kind)


def setup_inputs(seed: int = 0) -> dict:
    arg_keys = jax.random.split(jax.random.key(seed), 4)
    return {
        "activations": bell_draw_with(arg_keys[0], (IMAGES, CH, HEIGHT, WIDTH), 1.0, 16.0, ((0, 64), (2, 8)), (0, 1, 64, 4.0)),
        "out_grad": bell_draw_with(arg_keys[1], (IMAGES, CH, HEIGHT, WIDTH), 1.0, 6.0, ((0, 64), (2, 8)), (2, 1, 8, 2.0)),
        "kernel": centred(arg_keys[2], (CH, TAPS, CH), (9 * CH) ** -0.5, 0.109375, ((0, 64), (2, 8))),
    }


OFFSETS = ((-1, -1), (-1, 0), (-1, 1), (0, -1), (0, 0), (0, 1), (1, -1), (1, 0), (1, 1))

def reference(activations, out_grad, kernel):
    images = activations.shape[0]
    channels = activations.shape[1]
    height = activations.shape[2]
    row_len = activations.shape[3]
    grad_scale = 1.0 / math.sqrt(images * height * row_len)

    def per_image(summed, fields):
        act_image, grad_image = fields
        grad_padded = jnp.pad(grad_image, ((0, 0), (1, 1), (1, 1)))
        act_flat = act_image.reshape(channels, height * row_len)
        image_grad = jnp.zeros((channels, height * row_len), jnp.float32)
        for tap_index, (row_step, col_step) in enumerate(OFFSETS):
            shifted = grad_padded[:, 1 - row_step:1 - row_step + height, 1 - col_step:1 - col_step + row_len]
            shifted = shifted.reshape(channels, height * row_len)
            image_grad = image_grad + jnp.dot(kernel[:, tap_index, :], shifted, preferred_element_type=jnp.float32)
            partial_value = jnp.dot(act_flat, shifted.T, preferred_element_type=jnp.float32)
            summed = summed.at[:, tap_index, :].add(partial_value)
        return (summed, image_grad.reshape(channels, height, row_len).astype(jnp.bfloat16))
    start_sum = jnp.zeros((channels, 9, channels), jnp.float32)
    kernel_sum, input_grad = lax.scan(per_image, start_sum, (activations, out_grad))
    return (input_grad, kernel_sum * grad_scale)
```

```python
import math

import jax
import jax.numpy as jnp
import numpy as np
from jax import lax
from jax.experimental import pallas as pl
from jax.experimental.pallas import tpu as pltpu
from jax.sharding import PartitionSpec as P

MESH = pl.DeviceIdType.MESH
BF16 = jnp.bfloat16
F32 = jnp.float32

ROWS = 6
CH = 320
WIDTH = 128
NX, NY, NZ = 4, 8, 8
ZL = 4
KI = 5
KO = 40
HALF = CH // 2
NT = (((1,), (1,)), ((), ()))


def permutation():
    perm = np.zeros((CH, CH), np.float32)
    for core in range(2):
        for m in range(HALF):
            perm[core * HALF + m, 2 * KI * (m // KI) + KI * core + m % KI] = 1.0
    return perm


def spread():
    out = np.zeros((3 * HALF, 32 * 16), np.float32)
    for j in range(3):
        for m in range(HALF):
            out[j * HALF + m, 16 * (m // KI) + j * KI + m % KI] = 1.0
    return out


def fdot(a, b, dims=(((1,), (0,)), ((), ()))):
    return lax.dot_general(a, b, dims, preferred_element_type=F32)


def kernel(
    scale, act_hbm, grad_hbm, piece_ref, perm_hbm, permt_hbm, spread_hbm,
    ig_ref, kg_ref,
    act, gext, perm, permt, spr, amat, q, p, wp, wmat, igs, igr,
    rx1, rz1, s1a, s1b, rx2, rz2, s2, s2r, ry,
    lsem, psem, prec, hsem, hrec, fsem, frec, gsem, grec, xsem, xrec, zsem, zrec, x2sem, x2rec, z2sem, z2rec, ysem, yrec, isem, irec,
):
    band = lax.axis_index("band")
    strip = lax.axis_index("strip")
    core = lax.rem(band, 2)
    y = lax.rem(band // 2, NY)
    zl = band // (2 * NY)
    x = lax.rem(strip, NX)
    zh = strip // NX
    z = zh * ZL + zl

    def at(zz, yy, xx):
        zzh, zzl = zz // ZL, lax.rem(zz, ZL)
        return ((zzl * NY + yy) * 2 + core, zzh * NX + xx)

    pair = (band + 1 - 2 * core, strip)
    down = (band, lax.rem(strip + 1, 8))
    up = (band, lax.rem(strip + 7, 8))
    xs = [lax.rem(x + d, NX) for d in range(1, NX)]
    ys = [lax.rem(y + d, NY) for d in range(1, NY)]
    zs = [lax.rem(z + d, NZ) for d in range(1, NZ)]
    xdev = [at(z, y, v) for v in xs]
    ydev = [at(z, v, x) for v in ys]
    zdev = [at(v, y, x) for v in zs]

    barrier = pltpu.get_barrier_semaphore()
    partners = [pair, down, up] + xdev + ydev + zdev
    for dev in partners:
        pl.semaphore_signal(barrier, inc=1, device_id=dev, device_id_type=MESH)

    local = [
        pltpu.make_async_copy(act_hbm, act.at[0], lsem.at[0]),
        pltpu.make_async_copy(grad_hbm, gext.at[0, pl.ds(1, ROWS)], lsem.at[1]),
        pltpu.make_async_copy(perm_hbm, perm, lsem.at[2]),
        pltpu.make_async_copy(permt_hbm, permt, lsem.at[3]),
        pltpu.make_async_copy(spread_hbm, spr, lsem.at[4]),
        pltpu.make_async_copy(piece_ref, wp.at[zh, x, zl, y], lsem.at[5]),
    ]
    for c in local:
        c.start()
    s2r[...] = jnp.zeros_like(s2r)

    def remote(src, dst, ss, rs, dev):
        c = pltpu.make_async_remote_copy(
            src_ref=src, dst_ref=dst, send_sem=ss, recv_sem=rs, device_id=dev, device_id_type=MESH
        )
        c.start()
        return c

    pl.semaphore_wait(barrier, len(partners))
    sent = []
    halo = [
        remote(grad_hbm.at[ROWS - 1], gext.at[0, 0], hsem.at[0], hrec.at[0], down),
        remote(grad_hbm.at[0], gext.at[0, ROWS + 1], hsem.at[1], hrec.at[1], up),
    ]
    swap = [
        remote(grad_hbm, gext.at[1, pl.ds(1, ROWS)], psem.at[0], prec.at[0], pair),
        remote(act_hbm, act.at[1], psem.at[1], prec.at[1], pair),
    ]
    local[5].wait()
    gx = [
        remote(piece_ref, wp.at[zh, x, zl, y], gsem.at[i], grec.at[i], xdev[i])
        for i in range(NX - 1)
    ]
    sent += halo + swap + gx

    lane = lax.broadcasted_iota(jnp.int32, (80, WIDTH), 1)
    zero8 = jnp.zeros((8, WIDTH), F32)

    def fill(img, e, keep=None):
        col = pl.ds(pl.multiple_of((img * 8 + e) * WIDTH, WIDTH), WIDTH)
        for pr in range(4):
            g = gext[img, e, 80 * pr : 80 * pr + 80, :].astype(F32)
            if keep is not None:
                g = jnp.where(keep, g, 0.0)
            nxt = jnp.where(lane == WIDTH - 1, 0.0, pltpu.roll(g, WIDTH - 1, 1))
            prv = jnp.where(lane == 0, 0.0, pltpu.roll(g, 1, 1))
            for h in range(2):
                sl = slice(40 * h, 40 * h + 40)
                block = jnp.concatenate([nxt[sl], g[sl], prv[sl], zero8], axis=0)
                base = (2 * pr + h) * 128
                q[base : base + 128, col] = block.astype(BF16)

    def fill_image(img):
        @pl.loop(1, ROWS + 1)
        def _(e):
            fill(img, e)

    def rows_image(img):
        mine = perm[pl.ds(pl.multiple_of(core * HALF, HALF), HALF), :]
        for h in range(0, ROWS, 2):
            pairh = jnp.concatenate([act[img, h], act[img, h + 1]], axis=1)
            base = img * ROWS * WIDTH + h * WIDTH
            amat[:, base : base + 2 * WIDTH] = fdot(mine, pairh).astype(BF16)

    local[1].wait()
    fill_image(0)
    local[0].wait()
    local[2].wait()
    rows_image(0)
    swap[0].wait_recv()
    fill_image(1)
    swap[1].wait_recv()
    rows_image(1)

    for c in gx:
        c.wait_recv()
    gz = [
        remote(wp.at[zh, :, zl, y], wp.at[zh, :, zl, y], gsem.at[3 + i], grec.at[3 + i], zdev[i])
        for i in range(NZ - 1)
    ]
    sent += gz

    span = ROWS * WIDTH

    def partial(j):
        @pl.loop(0, 4)
        def _(n):
            rows = pl.ds(pl.multiple_of(n * 256, 256), 256)
            total = fdot(amat[:, 0:span], q[rows, (2 - j) * WIDTH : (2 - j) * WIDTH + span], NT)
            total = total + fdot(
                amat[:, span : 2 * span], q[rows, (10 - j) * WIDTH : (10 - j) * WIDTH + span], NT
            )
            for h in range(2):
                sidx = 2 * n + h
                p[j, sidx // NX, lax.rem(sidx, NX)] = total[:, 128 * h : 128 * h + 128].reshape(
                    ZL, HALF // ZL, 128
                )

    def send_x(j):
        return [
            remote(p.at[j, :, xs[i]], rx1.at[j - 1, i], xsem.at[j - 1, i], xrec.at[j - 1, i], xdev[i])
            for i in range(NX - 1)
        ]

    partial(1)
    x1 = {1: send_x(1)}

    for c in halo:
        c.wait_recv()
    forward = [
        remote(gext.at[0, e], gext.at[1, e], fsem.at[i], frec.at[i], pair)
        for i, e in enumerate((0, ROWS + 1))
    ]
    sent += forward
    top, bottom = strip > 0, strip < 7
    fill(0, 0, top)
    fill(0, ROWS + 1, bottom)
    forward[0].wait_recv()
    fill(1, 0, top)
    forward[1].wait_recv()
    fill(1, ROWS + 1, bottom)

    partial(0)
    z1 = [
        remote(
            p.at[0, zs[i] // ZL, :, lax.rem(zs[i], ZL)], rz1.at[i], zsem.at[i], zrec.at[i], zdev[i]
        )
        for i in range(NZ - 1)
    ]
    partial(2)
    x1[2] = send_x(2)
    sent += x1[1] + z1 + x1[2]

    for c in gz:
        c.wait_recv()
    gy = [
        remote(wp.at[:, :, :, y], wp.at[:, :, :, y], gsem.at[10 + i], grec.at[10 + i], ydev[i])
        for i in range(NY - 1)
    ]
    sent += gy

    z2 = {}

    def second(j):
        for c in x1[j]:
            c.wait_recv()
        for h in range(2):
            total = p[j, h, x]
            for i in range(NX - 1):
                total = total + rx1[j - 1, i, h]
            s1a[j - 1, h] = total
        z2[j] = [
            remote(
                s1a.at[j - 1, zs[i] // ZL, lax.rem(zs[i], ZL)],
                rz2.at[j - 1, i], z2sem.at[j - 1, i], z2rec.at[j - 1, i], zdev[i],
            )
            for i in range(NZ - 1)
        ]

    second(1)
    for c in z1:
        c.wait_recv()
    total = p[0, zh, :, zl]
    for i in range(NZ - 1):
        total = total + rz1[i]
    s1b[...] = total
    x2 = [
        remote(s1b.at[xs[i]], rx2.at[i], x2sem.at[i], x2rec.at[i], xdev[i]) for i in range(NX - 1)
    ]
    second(2)
    sent += x2 + z2[1] + z2[2]

    for j in (1, 2):
        for c in z2[j]:
            c.wait_recv()
        total = s1a[j - 1, zh, zl]
        for i in range(NZ - 1):
            total = total + rz2[j - 1, i]
        s2[j] = total
    for c in x2:
        c.wait_recv()
    total = s1b[x]
    for i in range(NX - 1):
        total = total + rx2[i]
    s2[0] = total
    for j in range(3):
        for v in range(NY):
            s2r[v, j, 0:KI, :] = s2[j, KI * v : KI * v + KI, :]
    y3 = [
        remote(s2r.at[ys[i]], ry.at[i], ysem.at[i], yrec.at[i], ydev[i]) for i in range(NY - 1)
    ]
    sent += y3

    for c in gy:
        c.wait_recv()
    local[4].wait()
    for pr in range(4):
        both = jnp.concatenate(
            [wp[(2 * pr + h) // NX, (2 * pr + h) % NX].reshape(512, 128) for h in range(2)], axis=1
        )
        wmat[:, 256 * pr : 256 * pr + 256] = fdot(spr[...], both).astype(BF16)

    def image(img, put):
        for h in range(0, ROWS, 2):
            total = None
            for j in range(3):
                base = (img * 8 + h + 2 - j) * WIDTH
                term = fdot(wmat[HALF * j : HALF * j + HALF, :], q[:, base : base + 256])
                total = term if total is None else total + term
            total = total.astype(BF16)
            put(h, total[:, :WIDTH])
            put(h + 1, total[:, WIDTH:])

    def put_peer(h, v):
        igs[h] = v

    def put_own(h, v):
        igr[h, pl.ds(pl.multiple_of(core * HALF, HALF), HALF), :] = v

    image(1, put_peer)
    half = pl.ds(pl.multiple_of(core * HALF, HALF), HALF)
    back = remote(igs, igr.at[:, half], isem, irec, pair)
    sent.append(back)
    image(0, put_own)
    local[3].wait()
    back.wait_recv()
    for h in range(0, ROWS, 2):
        both = jnp.concatenate([igr[h], igr[h + 1]], axis=1)
        out = fdot(permt[...], both).astype(BF16)
        ig_ref[h] = out[:, :WIDTH]
        ig_ref[h + 1] = out[:, WIDTH:]

    for c in y3:
        c.wait_recv()
    total = s2r[y]
    for i in range(NY - 1):
        total = total + ry[i]
    kg_ref[...] = total * scale
    for c in sent:
        c.wait_send()


def body(activations, out_grad, weights):
    cells = 64 * 48 * 128
    scale = 1.0 / math.sqrt(cells)
    act = jnp.transpose(activations[0], (1, 0, 2))
    grad = jnp.transpose(out_grad[0], (1, 0, 2))
    piece = jnp.transpose(weights.reshape(KI, 3, 3, KO), (1, 0, 2, 3)).reshape(3 * KI, 3 * KO)
    piece = jnp.pad(piece, ((0, 1), (0, 8)))
    perm = permutation()
    hbm = pl.BlockSpec(memory_space=pl.ANY)
    vmem = pl.BlockSpec(memory_space=pltpu.VMEM)
    V = pltpu.VMEM
    D = pltpu.SemaphoreType.DMA

    def run(*args):
        kernel(scale, *args)

    ig, kg = pl.pallas_call(
        run,
        out_shape=(
            jax.ShapeDtypeStruct((ROWS, CH, WIDTH), BF16),
            jax.ShapeDtypeStruct((3, 8, 128), F32),
        ),
        in_specs=[hbm, hbm, vmem, hbm, hbm, hbm],
        out_specs=(vmem, vmem),
        scratch_shapes=[
            V((2, ROWS, CH, WIDTH), BF16),
            V((2, 8, CH, WIDTH), BF16),
            V((CH, CH), BF16),
            V((CH, CH), BF16),
            V((3 * HALF, 512), BF16),
            V((HALF, 2 * ROWS * WIDTH), BF16),
            V((1024, 2048), BF16),
            V((3, 2, NX, ZL, 40, 128), F32),
            V((2, NX, ZL, NY, 16, 128), BF16),
            V((3 * HALF, 1024), BF16),
            V((ROWS, HALF, WIDTH), BF16),
            V((ROWS, CH, WIDTH), BF16),
            V((2, NX - 1, 2, ZL, 40, 128), F32),
            V((NZ - 1, NX, 40, 128), F32),
            V((2, 2, ZL, 40, 128), F32),
            V((NX, 40, 128), F32),
            V((NX - 1, 40, 128), F32),
            V((2, NZ - 1, 40, 128), F32),
            V((3, 40, 128), F32),
            V((NY, 3, 8, 128), F32),
            V((NY - 1, 3, 8, 128), F32),
            D((6,)), D((2,)), D((2,)), D((2,)), D((2,)), D((2,)), D((2,)), D((17,)), D((17,)),
            D((2, 3)), D((2, 3)), D((7,)), D((7,)), D((3,)), D((3,)), D((2, 7)), D((2, 7)),
            D((7,)), D((7,)), D(()), D(()),
        ],
        compiler_params=pltpu.CompilerParams(
            collective_id=0, has_side_effects=True, vmem_limit_bytes=48 << 20
        ),
    )(
        act, grad, piece,
        jnp.asarray(perm, BF16), jnp.asarray(perm.T, BF16), jnp.asarray(spread(), BF16),
    )
    input_grad = jnp.transpose(ig, (1, 0, 2))[None]
    kg = kg[:, :KI, : 3 * KO].reshape(3, KI, 3, KO)
    kernel_grad = jnp.transpose(kg, (1, 0, 2, 3)).reshape(KI, 9, KO)
    return input_grad, kernel_grad


def solution(mesh):
    in_specs = (
        P("band", None, "strip", None),
        P("band", None, "strip", None),
        P("band", None, "strip"),
    )
    out_specs = (P("band", None, "strip", None), P("band", None, "strip"))
    return jax.shard_map(body, mesh=mesh, in_specs=in_specs, out_specs=out_specs, check_vma=False)
```

```python
import math

import jax
import jax.numpy as jnp
import numpy as np
from jax import lax
from jax.experimental import pallas as pl
from jax.experimental.pallas import tpu as pltpu
from jax.sharding import PartitionSpec as P

MESH = pl.DeviceIdType.MESH
BF16 = jnp.bfloat16
F32 = jnp.float32

ROWS = 6
CH = 320
WIDTH = 128
NX, NY, NZ = 4, 8, 8
ZL = 4
KI = 5
KO = 40
HALF = CH // 2
NT = (((1,), (1,)), ((), ()))


def permutation():
    perm = np.zeros((CH, CH), np.float32)
    gather = np.zeros((2, 352, CH), np.float32)
    for core in range(2):
        for m in range(HALF):
            zy, k = m // KI, m % KI
            i = 2 * KI * zy + KI * core + k
            perm[i, core * HALF + m] = 1.0
            gather[core, m, i] = 1.0
            gather[core, HALF + 24 * (zy % NY) + KI * (zy // NY) + k, i] = 1.0
    return gather, perm


def spread():
    out = np.zeros((3 * HALF, 32 * 16), np.float32)
    for j in range(3):
        for m in range(HALF):
            out[j * HALF + m, 16 * (m // KI) + j * KI + m % KI] = 1.0
    return out


def fdot(a, b, dims=(((1,), (0,)), ((), ()))):
    return lax.dot_general(a, b, dims, preferred_element_type=F32)


def kernel(
    scale, act_hbm, grad_hbm, piece_ref, gather_hbm, permt_hbm, spread_hbm,
    ig_ref, kg_ref,
    act, gext, gather, permt, spr, amat, q, p, p2, wp, wmat, igs, igr,
    rx1, rz1, ry1, s1a, s1b, s1c, rx2, rx3, rz2, s2, s2r, ry, t2, t2r, rz3,
    lsem, psem, prec, hsem, hrec, fsem, frec, gsem, grec, xsem, xrec, zsem, zrec, rsem, rrec,
    x2sem, x2rec, x3sem, x3rec, z2sem, z2rec, ysem, yrec, z3sem, z3rec, isem, irec,
):
    band = lax.axis_index("band")
    strip = lax.axis_index("strip")
    core = lax.rem(band, 2)
    y = lax.rem(band // 2, NY)
    zl = band // (2 * NY)
    x = lax.rem(strip, NX)
    zh = strip // NX
    z = zh * ZL + zl

    def at(zz, yy, xx):
        zzh, zzl = zz // ZL, lax.rem(zz, ZL)
        return ((zzl * NY + yy) * 2 + core, zzh * NX + xx)

    pair = (band + 1 - 2 * core, strip)
    down = (band, lax.rem(strip + 1, 8))
    up = (band, lax.rem(strip + 7, 8))
    xs = [lax.rem(x + d, NX) for d in range(1, NX)]
    ys = [lax.rem(y + d, NY) for d in range(1, NY)]
    zs = [lax.rem(z + d, NZ) for d in range(1, NZ)]
    xdev = [at(z, y, v) for v in xs]
    ydev = [at(z, v, x) for v in ys]
    zdev = [at(v, y, x) for v in zs]

    barrier = pltpu.get_barrier_semaphore()
    partners = [pair, down, up] + xdev + ydev + zdev
    for dev in partners:
        pl.semaphore_signal(barrier, inc=1, device_id=dev, device_id_type=MESH)

    local = [
        pltpu.make_async_copy(grad_hbm, gext.at[0, pl.ds(1, ROWS)], lsem.at[1]),
        pltpu.make_async_copy(act_hbm, act.at[0], lsem.at[0]),
        pltpu.make_async_copy(gather_hbm.at[core], gather, lsem.at[2]),
        pltpu.make_async_copy(permt_hbm, permt, lsem.at[3]),
        pltpu.make_async_copy(spread_hbm, spr, lsem.at[4]),
        pltpu.make_async_copy(piece_ref.at[0], wp.at[0, zh, x, zl, y], lsem.at[5]),
        pltpu.make_async_copy(piece_ref.at[1], wp.at[1, zh, x, zl, y], lsem.at[6]),
    ]
    for c in local:
        c.start()
    s2r[...] = jnp.zeros_like(s2r)
    t2r[...] = jnp.zeros_like(t2r)

    sent = []

    def remote(src, dst, ss, rs, dev):
        c = pltpu.make_async_remote_copy(
            src_ref=src, dst_ref=dst, send_sem=ss, recv_sem=rs, device_id=dev, device_id_type=MESH
        )
        c.start()
        sent.append(c)
        return c

    def received(copies):
        for c in copies:
            c.wait_recv()

    pl.semaphore_wait(barrier, len(partners))
    halo = [
        remote(grad_hbm.at[ROWS - 1], gext.at[0, 0], hsem.at[0], hrec.at[0], down),
        remote(grad_hbm.at[0], gext.at[0, ROWS + 1], hsem.at[1], hrec.at[1], up),
    ]
    here = (zh, x, zl, y)
    gx = [
        remote(piece_ref.at[1], wp.at[(1, *here)], gsem.at[i], grec.at[i], xdev[i])
        for i in range(3)
    ]
    gy = [
        remote(piece_ref.at[0], wp.at[(0, *here)], gsem.at[3 + i], grec.at[3 + i], ydev[i])
        for i in range(7)
    ]
    swap = [
        remote(grad_hbm, gext.at[1, pl.ds(1, ROWS)], psem.at[0], prec.at[0], pair),
        remote(act_hbm, act.at[1], psem.at[1], prec.at[1], pair),
    ]

    lane = lax.broadcasted_iota(jnp.int32, (80, WIDTH), 1)
    zero8 = jnp.zeros((8, WIDTH), F32)

    def fill(img, e, keep=None):
        col = pl.ds(pl.multiple_of((img * 8 + e) * WIDTH, WIDTH), WIDTH)
        for pr in range(4):
            g = gext[img, e, 80 * pr : 80 * pr + 80, :].astype(F32)
            if keep is not None:
                g = jnp.where(keep, g, 0.0)
            nxt = jnp.where(lane == WIDTH - 1, 0.0, pltpu.roll(g, WIDTH - 1, 1))
            prv = jnp.where(lane == 0, 0.0, pltpu.roll(g, 1, 1))
            for h in range(2):
                sl = slice(40 * h, 40 * h + 40)
                block = jnp.concatenate([nxt[sl], g[sl], prv[sl], zero8], axis=0)
                base = (2 * pr + h) * 128
                q[base : base + 128, col] = block.astype(BF16)

    def fill_image(img):
        @pl.loop(1, ROWS + 1)
        def _(e):
            fill(img, e)

    def rows_image(img):
        for h in range(0, ROWS, 2):
            both = jnp.concatenate([act[img, h], act[img, h + 1]], axis=1)
            base = img * ROWS * WIDTH + h * WIDTH
            amat[:, base : base + 2 * WIDTH] = fdot(gather[...], both).astype(BF16)

    local[0].wait()
    fill_image(0)
    local[1].wait()
    local[2].wait()
    rows_image(0)

    received(gx)
    local[6].wait()
    gz1 = [
        remote(wp.at[1, zh, :, zl, y], wp.at[1, zh, :, zl, y], gsem.at[10 + i], grec.at[10 + i], zdev[i])
        for i in range(7)
    ]
    received(gy)
    local[5].wait()
    gz0 = [
        remote(wp.at[0, zh, x, zl], wp.at[0, zh, x, zl], gsem.at[17 + i], grec.at[17 + i], zdev[i])
        for i in range(7)
    ]

    swap[0].wait_recv()
    fill_image(1)
    received(halo)
    forward = [
        remote(gext.at[0, e], gext.at[1, e], fsem.at[i], frec.at[i], pair)
        for i, e in enumerate((0, ROWS + 1))
    ]
    swap[1].wait_recv()
    rows_image(1)

    span = ROWS * WIDTH

    def partial(j):
        rows_a = slice(0, HALF) if j < 2 else slice(HALF, 352)

        @pl.loop(0, 4)
        def _(n):
            rows = pl.ds(pl.multiple_of(n * 256, 256), 256)
            total = fdot(amat[rows_a, 0:span], q[rows, (2 - j) * WIDTH : (2 - j) * WIDTH + span], NT)
            total = total + fdot(
                amat[rows_a, span : 2 * span], q[rows, (10 - j) * WIDTH : (10 - j) * WIDTH + span], NT
            )
            for h in range(2):
                sidx = 2 * n + h
                one = total[:, 128 * h : 128 * h + 128]
                if j < 2:
                    p[j, sidx // NX, lax.rem(sidx, NX)] = one.reshape(ZL, 40, 128)
                else:
                    p2[sidx // NX, lax.rem(sidx, NX)] = one.reshape(NY, 24, 128)

    partial(1)
    x1 = [
        remote(p.at[1, :, xs[i]], rx1.at[i], xsem.at[i], xrec.at[i], xdev[i]) for i in range(NX - 1)
    ]

    received(gz1)
    gy1 = [
        remote(wp.at[1, :, :, :, y], wp.at[1, :, :, :, y], gsem.at[24 + i], grec.at[24 + i], ydev[i])
        for i in range(7)
    ]
    received(gz0)
    gx0 = [
        remote(wp.at[0, :, x], wp.at[0, :, x], gsem.at[31 + i], grec.at[31 + i], xdev[i])
        for i in range(3)
    ]

    top, bottom = strip > 0, strip < 7
    fill(0, 0, top)
    fill(0, ROWS + 1, bottom)
    forward[0].wait_recv()
    fill(1, 0, top)
    forward[1].wait_recv()
    fill(1, ROWS + 1, bottom)

    flows = ((1, 0, 4), (-1, 0, 3), (1, 1, 3), (-1, 1, 4))

    def ring(me, own, slots, ss, rs, devs):
        def send(f, k, src):
            sign = flows[f][0]
            return remote(src, slots.at[f, k], ss.at[f, k], rs.at[f, k], devs[0 if sign > 0 else 6])

        hops = {}

        def start():
            for f, (sign, part, steps) in enumerate(flows):
                dest = lax.rem(me + 8 + sign * steps, 8)
                hops[f, 0] = send(f, 0, own(dest, part))

        def step(k):
            for f, (sign, part, steps) in enumerate(flows):
                if k < steps:
                    hops[f, k - 1].wait_recv()
                    dest = lax.rem(me + 8 + sign * (steps - k), 8)
                    slots[f, k - 1] = slots[f, k - 1] + own(dest, part)[...]
                    hops[f, k] = send(f, k, slots.at[f, k - 1])

        def finish(part):
            total = own(me, part)[...]
            for f, (sign, fpart, steps) in enumerate(flows):
                if fpart == part:
                    hops[f, steps - 1].wait_recv()
                    total = total + slots[f, steps - 1]
            return total

        return start, step, finish

    def own_z(dest, part):
        return p.at[0, dest // ZL, pl.ds(2 * part, 2), lax.rem(dest, ZL)]

    def own_y(dest, part):
        return p2.at[part, :, dest]

    zstart, zstep, zfinish = ring(z, own_z, rz1, zsem, zrec, zdev)
    ystart, ystep, yfinish = ring(y, own_y, ry1, rsem, rrec, ydev)

    partial(0)
    zstart()
    partial(2)
    ystart()
    for k in range(1, 4):
        zstep(k)
        ystep(k)

    received(x1)
    for h in range(2):
        total = p[1, h, x]
        for i in range(NX - 1):
            total = total + rx1[i, h]
        s1a[h] = total
    z2 = [
        remote(s1a.at[zs[i] // ZL, lax.rem(zs[i], ZL)], rz2.at[i], z2sem.at[i], z2rec.at[i], zdev[i])
        for i in range(NZ - 1)
    ]
    for part in range(2):
        s1b[2 * part : 2 * part + 2] = zfinish(part)
    x2 = [
        remote(s1b.at[xs[i]], rx2.at[i], x2sem.at[i], x2rec.at[i], xdev[i]) for i in range(NX - 1)
    ]
    for part in range(2):
        s1c[part] = yfinish(part)
    x3 = [
        remote(s1c.at[:, xs[i]], rx3.at[i], x3sem.at[i], x3rec.at[i], xdev[i]) for i in range(NX - 1)
    ]

    received(gx0)
    received(gy1)
    local[4].wait()
    for pr in range(4):
        cols = []
        for sidx in (2 * pr, 2 * pr + 1):
            halves = [
                wp[half, sidx // NX, sidx % NX].astype(F32).reshape(32, 8, 128) for half in range(2)
            ]
            cols.append(jnp.concatenate(halves, axis=1).reshape(512, 128).astype(BF16))
        both = jnp.concatenate(cols, axis=1)
        wmat[:, 256 * pr : 256 * pr + 256] = fdot(spr[...], both).astype(BF16)

    def image(img, put):
        for h in range(0, ROWS, 2):
            total = None
            for j in range(3):
                base = (img * 8 + h + 2 - j) * WIDTH
                term = fdot(wmat[HALF * j : HALF * j + HALF, :], q[:, base : base + 256])
                total = term if total is None else total + term
            total = total.astype(BF16)
            put(h, total[:, :WIDTH])
            put(h + 1, total[:, WIDTH:])

    mine = pl.ds(pl.multiple_of(core * HALF, HALF), HALF)

    def put_peer(h, v):
        igs[h] = v

    def put_own(h, v):
        igr[h, mine, :] = v

    image(1, put_peer)
    back = remote(igs, igr.at[:, mine], isem, irec, pair)

    received(x2)
    total = s1b[x]
    for i in range(NX - 1):
        total = total + rx2[i]
    s2[0] = total
    received(x3)
    total = s1c[:, x]
    for i in range(NX - 1):
        total = total + rx3[i]
    t2[...] = total
    for h in range(2):
        for v in range(ZL):
            t2r[h, v, 0:KI, :] = t2[h, KI * v : KI * v + KI, :]
    z3 = [
        remote(t2r.at[zs[i] // ZL, lax.rem(zs[i], ZL)], rz3.at[i], z3sem.at[i], z3rec.at[i], zdev[i])
        for i in range(NZ - 1)
    ]
    received(z2)
    total = s1a[zh, zl]
    for i in range(NZ - 1):
        total = total + rz2[i]
    s2[1] = total
    for j in range(2):
        for v in range(NY):
            s2r[v, j, 0:KI, :] = s2[j, KI * v : KI * v + KI, :]
    y3 = [
        remote(s2r.at[ys[i]], ry.at[i], ysem.at[i], yrec.at[i], ydev[i]) for i in range(NY - 1)
    ]

    image(0, put_own)
    local[3].wait()
    back.wait_recv()
    for h in range(0, ROWS, 2):
        both = jnp.concatenate([igr[h], igr[h + 1]], axis=1)
        out = fdot(permt[...], both).astype(BF16)
        ig_ref[h] = out[:, :WIDTH]
        ig_ref[h + 1] = out[:, WIDTH:]

    received(z3)
    total = t2r[zh, zl]
    for i in range(NZ - 1):
        total = total + rz3[i]
    kg_ref[2] = total * scale
    received(y3)
    total = s2r[y]
    for i in range(NY - 1):
        total = total + ry[i]
    kg_ref[0:2] = total * scale
    for c in sent:
        c.wait_send()


def body(activations, out_grad, weights):
    cells = 64 * 48 * 128
    scale = 1.0 / math.sqrt(cells)
    act = jnp.transpose(activations[0], (1, 0, 2))
    grad = jnp.transpose(out_grad[0], (1, 0, 2))
    piece = jnp.transpose(weights.reshape(KI, 3, 3, KO), (1, 0, 2, 3)).reshape(3 * KI, 3 * KO)
    piece = jnp.pad(piece, ((0, 1), (0, 8))).reshape(2, 8, 128)
    gather, perm = permutation()
    hbm = pl.BlockSpec(memory_space=pltpu.HBM)
    vmem = pl.BlockSpec(memory_space=pltpu.VMEM)
    V = pltpu.VMEM
    D = pltpu.SemaphoreType.DMA

    def run(*args):
        kernel(scale, *args)

    ig, kg = pl.pallas_call(
        run,
        out_shape=(
            jax.ShapeDtypeStruct((ROWS, CH, WIDTH), BF16),
            jax.ShapeDtypeStruct((3, 8, 128), F32),
        ),
        in_specs=[hbm, hbm, vmem, hbm, hbm, hbm],
        out_specs=(vmem, vmem),
        scratch_shapes=[
            V((2, ROWS, CH, WIDTH), BF16),
            V((2, 8, CH, WIDTH), BF16),
            V((352, CH), BF16),
            V((CH, CH), BF16),
            V((3 * HALF, 512), BF16),
            V((352, 2 * ROWS * WIDTH), BF16),
            V((1024, 2048), BF16),
            V((2, 2, NX, ZL, 40, 128), F32),
            V((2, NX, NY, 24, 128), F32),
            V((2, 2, NX, ZL, NY, 8, 128), BF16),
            V((3 * HALF, 1024), BF16),
            V((ROWS, HALF, WIDTH), BF16),
            V((ROWS, CH, WIDTH), BF16),
            V((NX - 1, 2, ZL, 40, 128), F32),
            V((4, 4, 2, 40, 128), F32),
            V((4, 4, NX, 24, 128), F32),
            V((2, ZL, 40, 128), F32),
            V((NX, 40, 128), F32),
            V((2, NX, 24, 128), F32),
            V((NX - 1, 40, 128), F32),
            V((NX - 1, 2, 24, 128), F32),
            V((NZ - 1, 40, 128), F32),
            V((2, 40, 128), F32),
            V((NY, 2, 8, 128), F32),
            V((NY - 1, 2, 8, 128), F32),
            V((2, 24, 128), F32),
            V((2, ZL, 8, 128), F32),
            V((NZ - 1, 8, 128), F32),
            D((7,)), D((2,)), D((2,)), D((2,)), D((2,)), D((2,)), D((2,)), D((34,)), D((34,)),
            D((3,)), D((3,)), D((4, 4)), D((4, 4)), D((4, 4)), D((4, 4)),
            D((3,)), D((3,)), D((3,)), D((3,)), D((7,)), D((7,)), D((7,)), D((7,)), D((7,)), D((7,)),
            D(()), D(()),
        ],
        compiler_params=pltpu.CompilerParams(
            collective_id=0, has_side_effects=True, vmem_limit_bytes=60 << 20
        ),
    )(
        act, grad, piece,
        jnp.asarray(gather, BF16), jnp.asarray(perm, BF16), jnp.asarray(spread(), BF16),
    )
    input_grad = jnp.transpose(ig, (1, 0, 2))[None]
    kg = kg[:, :KI, : 3 * KO].reshape(3, KI, 3, KO)
    kernel_grad = jnp.transpose(kg, (1, 0, 2, 3)).reshape(KI, 9, KO)
    return input_grad, kernel_grad


def solution(mesh):
    in_specs = (
        P("band", None, "strip", None),
        P("band", None, "strip", None),
        P("band", None, "strip"),
    )
    out_specs = (P("band", None, "strip", None), P("band", None, "strip"))
    return jax.shard_map(body, mesh=mesh, in_specs=in_specs, out_specs=out_specs, check_vma=False)
```

```python
import math

import jax
import jax.numpy as jnp
import numpy as np
from jax import lax
from jax.experimental import pallas as pl
from jax.experimental.pallas import tpu as pltpu
from jax.sharding import PartitionSpec as P

MESH = pl.DeviceIdType.MESH
BF16 = jnp.bfloat16
F32 = jnp.float32

ROWS = 6
CH = 320
WIDTH = 128
NX, NY, NZ = 4, 8, 8
ZL = 4
KI = 5
KO = 40
HALF = CH // 2
NT = (((1,), (1,)), ((), ()))


def row_order():
    rows = {0: [], 1: [], 2: []}
    for y in range(NY):
        for k in range(4):
            rows[1] += [(zl, y, k) for zl in range(ZL)]
    for zl in range(ZL):
        rows[1] += [(zl, y, 4) for y in range(NY)]
    for ks in ((0, 1), (2, 3, 4)):
        for zl in range(ZL):
            for k in ks:
                rows[0] += [(zl, y, k) for y in range(NY)]
    for zl in range(ZL):
        for k in (0, 1, 2):
            rows[2] += [(zl, y, k) for y in range(NY)]
    for y in range(NY):
        for k in (3, 4):
            rows[2] += [(zl, y, k) for zl in range(ZL)]
    return rows[0] + rows[1] + rows[2]


def permutation():
    perm = np.zeros((CH, CH), np.float32)
    gather = np.zeros((2, 3 * HALF, CH), np.float32)
    for core in range(2):
        for m in range(HALF):
            perm[2 * KI * (m // KI) + KI * core + m % KI, core * HALF + m] = 1.0
        for m, (zl, y, k) in enumerate(row_order()):
            gather[core, m, 2 * KI * (zl * NY + y) + KI * core + k] = 1.0
    return gather, perm


def spread():
    out = np.zeros((3 * HALF, 32 * 16), np.float32)
    for j in range(3):
        for m in range(HALF):
            out[j * HALF + m, 16 * (m // KI) + j * KI + m % KI] = 1.0
    return out


def fdot(a, b, dims=(((1,), (0,)), ((), ()))):
    return lax.dot_general(a, b, dims, preferred_element_type=F32)


def kernel(
    scale, act_hbm, grad_hbm, piece_ref, gather_hbm, permt_hbm, spread_hbm,
    ig_ref, kg_ref,
    act, gext, gather, permt, spr, amat, q, wp, wmat, igs, igr,
    pxe, pxl, pze, pzl, py, rxe, rxl, rze, rzl, ry1,
    sxe, sxl, sz, sy, ry2, rz2, rx2, rx3, ty, tyr, ry3, tz, tzr, rz3,
    lsem, psem, prec, hsem, hrec, fsem, frec, gsem, grec, xsem, xrec, zsem, zrec, y1sem, y1rec,
    y2sem, y2rec, z2sem, z2rec, x2sem, x2rec, x3sem, x3rec, y3sem, y3rec, z3sem, z3rec, isem, irec,
):
    band = lax.axis_index("band")
    strip = lax.axis_index("strip")
    core = lax.rem(band, 2)
    y = lax.rem(band // 2, NY)
    zl = band // (2 * NY)
    x = lax.rem(strip, NX)
    zh = strip // NX
    z = zh * ZL + zl

    def at(zz, yy, xx):
        zzh, zzl = zz // ZL, lax.rem(zz, ZL)
        return ((zzl * NY + yy) * 2 + core, zzh * NX + xx)

    pair = (band + 1 - 2 * core, strip)
    down = (band, lax.rem(strip + 1, 8))
    up = (band, lax.rem(strip + 7, 8))
    xs = [lax.rem(x + d, NX) for d in range(1, NX)]
    ys = [lax.rem(y + d, NY) for d in range(1, NY)]
    zs = [lax.rem(z + d, NZ) for d in range(1, NZ)]
    xdev = [at(z, y, v) for v in xs]
    ydev = [at(z, v, x) for v in ys]
    zdev = [at(v, y, x) for v in zs]

    barrier = pltpu.get_barrier_semaphore()
    partners = [pair, down, up] + xdev + ydev + zdev
    for dev in partners:
        pl.semaphore_signal(barrier, inc=1, device_id=dev, device_id_type=MESH)

    local = [
        pltpu.make_async_copy(grad_hbm, gext.at[0, pl.ds(1, ROWS)], lsem.at[1]),
        pltpu.make_async_copy(act_hbm, act.at[0], lsem.at[0]),
        pltpu.make_async_copy(gather_hbm.at[core], gather, lsem.at[2]),
        pltpu.make_async_copy(permt_hbm, permt, lsem.at[3]),
        pltpu.make_async_copy(spread_hbm, spr, lsem.at[4]),
        pltpu.make_async_copy(piece_ref.at[0], wp.at[0, zh, x, zl, y], lsem.at[5]),
        pltpu.make_async_copy(piece_ref.at[1], wp.at[1, zh, x, zl, y], lsem.at[6]),
    ]
    for c in local:
        c.start()
    tyr[...] = jnp.zeros_like(tyr)
    tzr[...] = jnp.zeros_like(tzr)
    kg_ref[...] = jnp.zeros_like(kg_ref)

    sent = []

    def remote(src, dst, ss, rs, dev):
        c = pltpu.make_async_remote_copy(
            src_ref=src, dst_ref=dst, send_sem=ss, recv_sem=rs, device_id=dev, device_id_type=MESH
        )
        c.start()
        sent.append(c)
        return c

    def received(copies):
        for c in copies:
            c.wait_recv()

    pl.semaphore_wait(barrier, len(partners))
    inner, outer = strip > 0, strip < 7
    halo_down = []
    halo_up = []
    for n in range(4):
        part = pl.ds(80 * n, 80)
        halo_down.append(
            pltpu.make_async_remote_copy(
                src_ref=grad_hbm.at[ROWS - 1, part], dst_ref=gext.at[0, 0, part],
                send_sem=hsem.at[0, n], recv_sem=hrec.at[0, n], device_id=down, device_id_type=MESH,
            )
        )
        halo_up.append(
            pltpu.make_async_remote_copy(
                src_ref=grad_hbm.at[0, part], dst_ref=gext.at[0, ROWS + 1, part],
                send_sem=hsem.at[1, n], recv_sem=hrec.at[1, n], device_id=up, device_id_type=MESH,
            )
        )

    @pl.when(outer)
    def _():
        for c in halo_down:
            c.start()

    @pl.when(inner)
    def _():
        for c in halo_up:
            c.start()

    here = (zh, x, zl, y)
    gx = [
        remote(piece_ref.at[1], wp.at[(1, *here)], gsem.at[i], grec.at[i], xdev[i])
        for i in range(3)
    ]
    gy = [
        remote(piece_ref.at[0], wp.at[(0, *here)], gsem.at[3 + i], grec.at[3 + i], ydev[i])
        for i in range(7)
    ]
    swap = [
        remote(grad_hbm, gext.at[1, pl.ds(1, ROWS)], psem.at[0], prec.at[0], pair),
        remote(act_hbm, act.at[1], psem.at[1], prec.at[1], pair),
    ]

    lane = lax.broadcasted_iota(jnp.int32, (80, WIDTH), 1)
    zero8 = jnp.zeros((8, WIDTH), F32)

    def fill(img, e, keep=None, parts=range(4)):
        col = pl.ds(pl.multiple_of((img * 8 + e) * WIDTH, WIDTH), WIDTH)
        for pr in parts:
            g = gext[img, e, 80 * pr : 80 * pr + 80, :].astype(F32)
            if keep is not None:
                g = jnp.where(keep, g, 0.0)
            nxt = jnp.where(lane == WIDTH - 1, 0.0, pltpu.roll(g, WIDTH - 1, 1))
            prv = jnp.where(lane == 0, 0.0, pltpu.roll(g, 1, 1))
            for h in range(2):
                sl = slice(40 * h, 40 * h + 40)
                block = jnp.concatenate([nxt[sl], g[sl], prv[sl], zero8], axis=0)
                base = (2 * pr + h) * 128
                q[base : base + 128, col] = block.astype(BF16)

    def fill_image(img):
        @pl.loop(1, ROWS + 1)
        def _(e):
            fill(img, e)

    def rows_image(img):
        for h in range(0, ROWS, 2):
            both = jnp.concatenate([act[img, h], act[img, h + 1]], axis=1)
            base = img * ROWS * WIDTH + h * WIDTH
            amat[:, base : base + 2 * WIDTH] = fdot(gather[...], both).astype(BF16)

    def forward(n):
        part = pl.ds(80 * n, 80)

        @pl.when(inner)
        def _():
            halo_down[n].wait_recv()

        @pl.when(outer)
        def _():
            halo_up[n].wait_recv()

        return [
            remote(gext.at[0, e, part], gext.at[1, e, part], fsem.at[i, n], frec.at[i, n], pair)
            for i, e in enumerate((0, ROWS + 1))
        ]

    local[0].wait()
    fill_image(0)
    received(gx)
    local[6].wait()
    gz1 = [
        remote(wp.at[1, zh, :, zl, y], wp.at[1, zh, :, zl, y], gsem.at[10 + i], grec.at[10 + i], zdev[i])
        for i in range(7)
    ]
    received(gy)
    local[5].wait()
    gz0 = [
        remote(wp.at[0, zh, x, zl], wp.at[0, zh, x, zl], gsem.at[17 + i], grec.at[17 + i], zdev[i])
        for i in range(7)
    ]
    local[1].wait()
    local[2].wait()
    rows_image(0)
    swap[0].wait_recv()
    fill_image(1)
    swap[1].wait_recv()
    rows_image(1)
    received(gz0)
    gx0 = [
        remote(wp.at[0, :, x], wp.at[0, :, x], gsem.at[31 + i], grec.at[31 + i], xdev[i])
        for i in range(3)
    ]
    received(gz1)
    gy1 = [
        remote(wp.at[1, :, :, :, y], wp.at[1, :, :, :, y], gsem.at[24 + i], grec.at[24 + i], ydev[i])
        for i in range(7)
    ]

    span = ROWS * WIDTH

    def product(j, n):
        rows = pl.ds(256 * n if isinstance(n, int) else pl.multiple_of(n * 256, 256), 256)
        mine = slice(HALF * j, HALF * j + HALF)
        total = fdot(amat[mine, 0:span], q[rows, (2 - j) * WIDTH : (2 - j) * WIDTH + span], NT)
        return total + fdot(
            amat[mine, span : 2 * span], q[rows, (10 - j) * WIDTH : (10 - j) * WIDTH + span], NT
        )

    @pl.loop(0, 4)
    def _(n):
        total = product(1, n)
        for h in range(2):
            sh, sx = n // 2, 2 * lax.rem(n, 2) + h
            one = total[:, 128 * h : 128 * h + 128]
            pxe[sh, sx] = one[:128].reshape(NY, 16, 128)
            pze[sh, sx] = one[128:].reshape(ZL, 8, 128)

    xe = [
        remote(pxe.at[:, xs[i]], rxe.at[i], xsem.at[0, i], xrec.at[0, i], xdev[i]) for i in range(3)
    ]
    ze = [
        remote(
            pze.at[zs[i] // ZL, :, lax.rem(zs[i], ZL)], rze.at[i], zsem.at[0, i], zrec.at[0, i], zdev[i]
        )
        for i in range(7)
    ]

    ahead = forward(0)
    for n in range(4):
        now = ahead
        if n < 3:
            ahead = forward(n + 1)
        fill(0, 0, inner, (n,))
        fill(0, ROWS + 1, outer, (n,))
        now[0].wait_recv()
        fill(1, 0, inner, (n,))
        now[1].wait_recv()
        fill(1, ROWS + 1, outer, (n,))
        first = product(0, n)
        third = product(2, n)
        for h in range(2):
            sh, sx = n // 2, 2 * (n % 2) + h
            one = first[:, 128 * h : 128 * h + 128]
            pxl[sh, sx, :, 0:16] = one[:64].reshape(ZL, 16, 128)
            pzl[sh, sx] = one[64:].reshape(ZL, 24, 128)
            one = third[:, 128 * h : 128 * h + 128]
            pxl[sh, sx, :, 16:40] = one[:96].reshape(ZL, 24, 128)
            py[sh, sx] = one[96:].reshape(NY, 8, 128)

    zlate = [
        remote(
            pzl.at[zs[i] // ZL, :, lax.rem(zs[i], ZL)], rzl.at[i], zsem.at[1, i], zrec.at[1, i], zdev[i]
        )
        for i in range(7)
    ]
    y1 = [remote(py.at[:, :, ys[i]], ry1.at[i], y1sem.at[i], y1rec.at[i], ydev[i]) for i in range(7)]
    xl = [
        remote(pxl.at[:, xs[i]], rxl.at[i], xsem.at[1, i], xrec.at[1, i], xdev[i]) for i in range(3)
    ]

    received(gx0)
    received(gy1)
    local[4].wait()
    for pr in range(4):
        cols = []
        for sidx in (2 * pr, 2 * pr + 1):
            halves = [
                wp[half, sidx // NX, sidx % NX].astype(F32).reshape(32, 8, 128) for half in range(2)
            ]
            cols.append(jnp.concatenate(halves, axis=1).reshape(512, 128).astype(BF16))
        both = jnp.concatenate(cols, axis=1)
        wmat[:, 256 * pr : 256 * pr + 256] = fdot(spr[...], both).astype(BF16)

    def image(img, put):
        for h in range(0, ROWS, 2):
            total = None
            for j in range(3):
                base = (img * 8 + h + 2 - j) * WIDTH
                term = fdot(wmat[HALF * j : HALF * j + HALF, :], q[:, base : base + 256])
                total = term if total is None else total + term
            total = total.astype(BF16)
            put(h, total[:, :WIDTH])
            put(h + 1, total[:, WIDTH:])

    mine = pl.ds(pl.multiple_of(core * HALF, HALF), HALF)

    def put_peer(h, v):
        igs[h] = v

    def put_own(h, v):
        igr[h, mine, :] = v

    image(1, put_peer)
    back = remote(igs, igr.at[:, mine], isem, irec, pair)

    image(0, put_own)

    received(xe)
    for h in range(2):
        total = pxe[h, x]
        for i in range(3):
            total = total + rxe[i, h]
        sxe[h] = total
    y2 = [remote(sxe.at[:, ys[i]], ry2.at[i], y2sem.at[i], y2rec.at[i], ydev[i]) for i in range(7)]
    received(y1)
    total = py[:, :, y]
    for i in range(7):
        total = total + ry1[i]
    sy[...] = total
    x3 = [remote(sy.at[:, xs[i]], rx3.at[i], x3sem.at[i], x3rec.at[i], xdev[i]) for i in range(3)]
    received(xl)
    for h in range(2):
        total = pxl[h, x]
        for i in range(3):
            total = total + rxl[i, h]
        sxl[h] = total
    z2 = [
        remote(sxl.at[zs[i] // ZL, lax.rem(zs[i], ZL)], rz2.at[i], z2sem.at[i], z2rec.at[i], zdev[i])
        for i in range(7)
    ]
    received(ze)
    received(zlate)
    early = pze[zh, :, zl]
    late = pzl[zh, :, zl]
    for i in range(7):
        early = early + rze[i]
        late = late + rzl[i]
    sz[:, 0:8] = early
    sz[:, 8:32] = late
    x2 = [remote(sz.at[xs[i]], rx2.at[i], x2sem.at[i], x2rec.at[i], xdev[i]) for i in range(3)]

    received(y2)
    total = sxe[:, y]
    for i in range(7):
        total = total + ry2[i]
    tz[:, 0:16] = total
    received(x3)
    total = sy[:, x]
    for i in range(3):
        total = total + rx3[i]
    tz[:, 16:24] = total
    for h in range(2):
        for v in range(ZL):
            for k in range(6):
                tzr[h, v, k : k + 1, :] = tz[h, ZL * k + v : ZL * k + v + 1, :]
    z3 = [
        remote(tzr.at[zs[i] // ZL, lax.rem(zs[i], ZL)], rz3.at[i], z3sem.at[i], z3rec.at[i], zdev[i])
        for i in range(7)
    ]
    received(z2)
    total = sxl[zh, zl]
    for i in range(7):
        total = total + rz2[i]
    ty[0:40] = total
    received(x2)
    total = sz[x]
    for i in range(3):
        total = total + rx2[i]
    ty[40:72] = total
    for v in range(NY):
        for k in range(9):
            tyr[v, k : k + 1, :] = ty[NY * k + v : NY * k + v + 1, :]
    y3 = [remote(tyr.at[ys[i]], ry3.at[i], y3sem.at[i], y3rec.at[i], ydev[i]) for i in range(7)]

    local[3].wait()
    back.wait_recv()
    for h in range(0, ROWS, 2):
        both = jnp.concatenate([igr[h], igr[h + 1]], axis=1)
        out = fdot(permt[...], both).astype(BF16)
        ig_ref[h] = out[:, :WIDTH]
        ig_ref[h + 1] = out[:, WIDTH:]

    received(z3)
    total = tzr[zh, zl]
    for i in range(7):
        total = total + rz3[i]
    total = total * scale
    kg_ref[1, 0:4] = total[0:4]
    kg_ref[2, 3:5] = total[4:6]
    received(y3)
    total = tyr[y]
    for i in range(7):
        total = total + ry3[i]
    total = total * scale
    kg_ref[0, 0:2] = total[0:2]
    kg_ref[2, 0:3] = total[2:5]
    kg_ref[1, 4:5] = total[5:6]
    kg_ref[0, 2:5] = total[6:9]
    for c in sent:
        c.wait_send()

    @pl.when(outer)
    def _():
        for c in halo_down:
            c.wait_send()

    @pl.when(inner)
    def _():
        for c in halo_up:
            c.wait_send()


def body(activations, out_grad, weights):
    cells = 64 * 48 * 128
    scale = 1.0 / math.sqrt(cells)
    act = jnp.transpose(activations[0], (1, 0, 2))
    grad = jnp.transpose(out_grad[0], (1, 0, 2))
    piece = jnp.transpose(weights.reshape(KI, 3, 3, KO), (1, 0, 2, 3)).reshape(3 * KI, 3 * KO)
    piece = jnp.pad(piece, ((0, 1), (0, 8))).reshape(2, 8, 128)
    gather, perm = permutation()
    hbm = pl.BlockSpec(memory_space=pltpu.HBM)
    vmem = pl.BlockSpec(memory_space=pltpu.VMEM)
    V = pltpu.VMEM
    D = pltpu.SemaphoreType.DMA

    def run(*args):
        kernel(scale, *args)

    ig, kg = pl.pallas_call(
        run,
        out_shape=(
            jax.ShapeDtypeStruct((ROWS, CH, WIDTH), BF16),
            jax.ShapeDtypeStruct((3, 8, 128), F32),
        ),
        in_specs=[hbm, hbm, vmem, hbm, hbm, hbm],
        out_specs=(vmem, vmem),
        scratch_shapes=[
            V((2, ROWS, CH, WIDTH), BF16),
            V((2, 8, CH, WIDTH), BF16),
            V((3 * HALF, CH), BF16),
            V((CH, CH), BF16),
            V((3 * HALF, 512), BF16),
            V((3 * HALF, 2 * ROWS * WIDTH), BF16),
            V((1024, 2048), BF16),
            V((2, 2, NX, ZL, NY, 8, 128), BF16),
            V((3 * HALF, 1024), BF16),
            V((ROWS, HALF, WIDTH), BF16),
            V((ROWS, CH, WIDTH), BF16),
            V((2, NX, NY, 16, 128), F32),
            V((2, NX, ZL, 40, 128), F32),
            V((2, NX, ZL, 8, 128), F32),
            V((2, NX, ZL, 24, 128), F32),
            V((2, NX, NY, 8, 128), F32),
            V((3, 2, NY, 16, 128), F32),
            V((3, 2, ZL, 40, 128), F32),
            V((7, NX, 8, 128), F32),
            V((7, NX, 24, 128), F32),
            V((7, 2, NX, 8, 128), F32),
            V((2, NY, 16, 128), F32),
            V((2, ZL, 40, 128), F32),
            V((NX, 32, 128), F32),
            V((2, NX, 8, 128), F32),
            V((7, 2, 16, 128), F32),
            V((7, 40, 128), F32),
            V((3, 32, 128), F32),
            V((3, 2, 8, 128), F32),
            V((72, 128), F32),
            V((NY, 16, 128), F32),
            V((7, 16, 128), F32),
            V((2, 24, 128), F32),
            V((2, ZL, 8, 128), F32),
            V((7, 8, 128), F32),
            D((7,)), D((2,)), D((2,)), D((2, 4)), D((2, 4)), D((2, 4)), D((2, 4)), D((34,)), D((34,)),
            D((2, 3)), D((2, 3)), D((2, 7)), D((2, 7)), D((7,)), D((7,)), D((7,)), D((7,)), D((7,)), D((7,)),
            D((3,)), D((3,)), D((3,)), D((3,)), D((7,)), D((7,)), D((7,)), D((7,)), D(()), D(()),
        ],
        compiler_params=pltpu.CompilerParams(
            collective_id=0, has_side_effects=True, vmem_limit_bytes=60 << 20
        ),
    )(
        act, grad, piece,
        jnp.asarray(gather, BF16), jnp.asarray(perm, BF16), jnp.asarray(spread(), BF16),
    )
    input_grad = jnp.transpose(ig, (1, 0, 2))[None]
    kg = kg[:, :KI, : 3 * KO].reshape(3, KI, 3, KO)
    kernel_grad = jnp.transpose(kg, (1, 0, 2, 3)).reshape(KI, 9, KO)
    return input_grad, kernel_grad


def solution(mesh):
    in_specs = (
        P("band", None, "strip", None),
        P("band", None, "strip", None),
        P("band", None, "strip"),
    )
    out_specs = (P("band", None, "strip", None), P("band", None, "strip"))
    return jax.shard_map(body, mesh=mesh, in_specs=in_specs, out_specs=out_specs, check_vma=False)
```

```python
import math

import jax
import jax.numpy as jnp
import numpy as np
from jax import lax
from jax.experimental import pallas as pl
from jax.experimental.pallas import tpu as pltpu
from jax.sharding import PartitionSpec as P

MESH = pl.DeviceIdType.MESH
BF16 = jnp.bfloat16
F32 = jnp.float32

ROWS = 6
CH = 320
WIDTH = 128
NX, NY, NZ = 4, 8, 8
ZL = 4
KI = 5
KO = 40
HALF = CH // 2
NT = (((1,), (1,)), ((), ()))


def row_order():
    rows = {0: [], 1: [], 2: []}
    for y in range(NY):
        for k in range(4):
            rows[1] += [(zl, y, k) for zl in range(ZL)]
    for zl in range(ZL):
        rows[1] += [(zl, y, 4) for y in range(NY)]
    for ks in ((0, 1), (2, 3, 4)):
        for zl in range(ZL):
            for k in ks:
                rows[0] += [(zl, y, k) for y in range(NY)]
    for zl in range(ZL):
        for k in (0, 1, 2):
            rows[2] += [(zl, y, k) for y in range(NY)]
    for y in range(NY):
        for k in (3, 4):
            rows[2] += [(zl, y, k) for zl in range(ZL)]
    return rows[0] + rows[1] + rows[2]


def permutation():
    perm = np.zeros((CH, CH), np.float32)
    gather = np.zeros((2, 3 * HALF, CH), np.float32)
    for core in range(2):
        for m in range(HALF):
            perm[2 * KI * (m // KI) + KI * core + m % KI, core * HALF + m] = 1.0
        for m, (zl, y, k) in enumerate(row_order()):
            gather[core, m, 2 * KI * (zl * NY + y) + KI * core + k] = 1.0
    return gather, perm


def spread():
    out = np.zeros((3 * HALF, 32 * 16), np.float32)
    for j in range(3):
        for m in range(HALF):
            out[j * HALF + m, 16 * (m // KI) + j * KI + m % KI] = 1.0
    return out


def fdot(a, b, dims=(((1,), (0,)), ((), ()))):
    return lax.dot_general(a, b, dims, preferred_element_type=F32)


def kernel(
    scale, act_hbm, grad_hbm, piece_ref, gather_hbm, permt_hbm, spread_hbm,
    ig_ref, kg_ref,
    act, gext, gather, permt, spr, amat, q, wp, wmat, igs, igr,
    pxe, pxl, pze, pzl, py, rxe, rxl, rze, rzl, ry1,
    sxe, sxl, sz, sy, ry2, rz2, rx2, rx3, ty, tyr, ry3, tz, tzr, rz3,
    lsem, psem, prec, hsem, hrec, fsem, frec, gsem, grec, xsem, xrec, zsem, zrec, y1sem, y1rec,
    y2sem, y2rec, z2sem, z2rec, x2sem, x2rec, x3sem, x3rec, y3sem, y3rec, z3sem, z3rec, isem, irec,
):
    band = lax.axis_index("band")
    strip = lax.axis_index("strip")
    core = lax.rem(band, 2)
    y = lax.rem(band // 2, NY)
    zl = band // (2 * NY)
    x = lax.rem(strip, NX)
    zh = strip // NX
    z = zh * ZL + zl

    def at(zz, yy, xx):
        zzh, zzl = zz // ZL, lax.rem(zz, ZL)
        return ((zzl * NY + yy) * 2 + core, zzh * NX + xx)

    pair = (band + 1 - 2 * core, strip)
    down = (band, lax.rem(strip + 1, 8))
    up = (band, lax.rem(strip + 7, 8))
    xs = [lax.rem(x + d, NX) for d in range(1, NX)]
    ys = [lax.rem(y + d, NY) for d in range(1, NY)]
    zs = [lax.rem(z + d, NZ) for d in range(1, NZ)]
    xdev = [at(z, y, v) for v in xs]
    ydev = [at(z, v, x) for v in ys]
    zdev = [at(v, y, x) for v in zs]

    barrier = pltpu.get_barrier_semaphore()
    partners = [pair, down, up] + xdev + ydev + zdev
    for dev in partners:
        pl.semaphore_signal(barrier, inc=1, device_id=dev, device_id_type=MESH)

    local = [
        pltpu.make_async_copy(grad_hbm, gext.at[0, pl.ds(1, ROWS)], lsem.at[1]),
        pltpu.make_async_copy(act_hbm, act.at[0], lsem.at[0]),
        pltpu.make_async_copy(gather_hbm.at[core], gather, lsem.at[2]),
        pltpu.make_async_copy(permt_hbm, permt, lsem.at[3]),
        pltpu.make_async_copy(spread_hbm, spr, lsem.at[4]),
        pltpu.make_async_copy(piece_ref.at[0], wp.at[0, zh, x, zl, y], lsem.at[5]),
        pltpu.make_async_copy(piece_ref.at[1], wp.at[1, zh, x, zl, y], lsem.at[6]),
    ]
    for c in local:
        c.start()
    tyr[...] = jnp.zeros_like(tyr)
    tzr[...] = jnp.zeros_like(tzr)
    kg_ref[...] = jnp.zeros_like(kg_ref)

    sent = []

    def remote(src, dst, ss, rs, dev):
        c = pltpu.make_async_remote_copy(
            src_ref=src, dst_ref=dst, send_sem=ss, recv_sem=rs, device_id=dev, device_id_type=MESH
        )
        c.start()
        sent.append(c)
        return c

    def received(copies):
        for c in copies:
            c.wait_recv()

    pl.semaphore_wait(barrier, len(partners))
    inner, outer = strip > 0, strip < 7
    halo_down = []
    halo_up = []
    for n in range(4):
        part = pl.ds(80 * n, 80)
        halo_down.append(
            pltpu.make_async_remote_copy(
                src_ref=grad_hbm.at[ROWS - 1, part], dst_ref=gext.at[0, 0, part],
                send_sem=hsem.at[0, n], recv_sem=hrec.at[0, n], device_id=down, device_id_type=MESH,
            )
        )
        halo_up.append(
            pltpu.make_async_remote_copy(
                src_ref=grad_hbm.at[0, part], dst_ref=gext.at[0, ROWS + 1, part],
                send_sem=hsem.at[1, n], recv_sem=hrec.at[1, n], device_id=up, device_id_type=MESH,
            )
        )

    @pl.when(outer)
    def _():
        for c in halo_down:
            c.start()

    @pl.when(inner)
    def _():
        for c in halo_up:
            c.start()

    here = (zh, x, zl, y)
    gx = [
        remote(piece_ref.at[1], wp.at[(1, *here)], gsem.at[i], grec.at[i], xdev[i])
        for i in range(3)
    ]
    gy = [
        remote(piece_ref.at[0], wp.at[(0, *here)], gsem.at[3 + i], grec.at[3 + i], ydev[i])
        for i in range(7)
    ]
    swap = [
        remote(grad_hbm, gext.at[1, pl.ds(1, ROWS)], psem.at[0], prec.at[0], pair),
        remote(act_hbm, act.at[1], psem.at[1], prec.at[1], pair),
    ]

    lane = lax.broadcasted_iota(jnp.int32, (80, WIDTH), 1)
    zero8 = jnp.zeros((8, WIDTH), F32)

    def fill(img, e, keep=None, parts=range(4)):
        col = pl.ds(pl.multiple_of((img * 8 + e) * WIDTH, WIDTH), WIDTH)
        for pr in parts:
            g = gext[img, e, 80 * pr : 80 * pr + 80, :].astype(F32)
            if keep is not None:
                g = jnp.where(keep, g, 0.0)
            nxt = jnp.where(lane == WIDTH - 1, 0.0, pltpu.roll(g, WIDTH - 1, 1))
            prv = jnp.where(lane == 0, 0.0, pltpu.roll(g, 1, 1))
            for h in range(2):
                sl = slice(40 * h, 40 * h + 40)
                block = jnp.concatenate([nxt[sl], g[sl], prv[sl], zero8], axis=0)
                base = (2 * pr + h) * 128
                q[base : base + 128, col] = block.astype(BF16)

    def fill_image(img):
        @pl.loop(1, ROWS + 1)
        def _(e):
            fill(img, e)

    def rows_image(img):
        for h in range(0, ROWS, 2):
            both = jnp.concatenate([act[img, h], act[img, h + 1]], axis=1)
            base = img * ROWS * WIDTH + h * WIDTH
            amat[:, base : base + 2 * WIDTH] = fdot(gather[...], both).astype(BF16)

    def forward(n):
        part = pl.ds(80 * n, 80)

        @pl.when(inner)
        def _():
            halo_down[n].wait_recv()

        @pl.when(outer)
        def _():
            halo_up[n].wait_recv()

        return [
            remote(gext.at[0, e, part], gext.at[1, e, part], fsem.at[i, n], frec.at[i, n], pair)
            for i, e in enumerate((0, ROWS + 1))
        ]

    local[0].wait()
    fill_image(0)
    local[1].wait()
    local[2].wait()
    rows_image(0)
    swap[0].wait_recv()
    fill_image(1)
    swap[1].wait_recv()
    rows_image(1)
    span = ROWS * WIDTH

    def product(j, n):
        rows = pl.ds(256 * n if isinstance(n, int) else pl.multiple_of(n * 256, 256), 256)
        mine = slice(HALF * j, HALF * j + HALF)
        total = fdot(amat[mine, 0:span], q[rows, (2 - j) * WIDTH : (2 - j) * WIDTH + span], NT)
        return total + fdot(
            amat[mine, span : 2 * span], q[rows, (10 - j) * WIDTH : (10 - j) * WIDTH + span], NT
        )

    @pl.loop(0, 4)
    def _(n):
        total = product(1, n)
        for h in range(2):
            sh, sx = n // 2, 2 * lax.rem(n, 2) + h
            one = total[:, 128 * h : 128 * h + 128]
            pxe[sh, sx] = one[:128].reshape(NY, 16, 128)
            pze[sh, sx] = one[128:].reshape(ZL, 8, 128)

    xe = [
        remote(pxe.at[:, xs[i]], rxe.at[i], xsem.at[0, i], xrec.at[0, i], xdev[i]) for i in range(3)
    ]
    ze = [
        remote(
            pze.at[zs[i] // ZL, :, lax.rem(zs[i], ZL)], rze.at[i], zsem.at[0, i], zrec.at[0, i], zdev[i]
        )
        for i in range(7)
    ]

    received(gx)
    local[6].wait()
    gz1 = [
        remote(wp.at[1, zh, :, zl, y], wp.at[1, zh, :, zl, y], gsem.at[10 + i], grec.at[10 + i], zdev[i])
        for i in range(7)
    ]
    received(gy)
    local[5].wait()
    gz0 = [
        remote(wp.at[0, zh, x, zl], wp.at[0, zh, x, zl], gsem.at[17 + i], grec.at[17 + i], zdev[i])
        for i in range(7)
    ]
    ahead = forward(0)
    for n in range(4):
        now = ahead
        if n < 3:
            ahead = forward(n + 1)
        fill(0, 0, inner, (n,))
        fill(0, ROWS + 1, outer, (n,))
        now[0].wait_recv()
        fill(1, 0, inner, (n,))
        now[1].wait_recv()
        fill(1, ROWS + 1, outer, (n,))
        first = product(0, n)
        third = product(2, n)
        for h in range(2):
            sh, sx = n // 2, 2 * (n % 2) + h
            one = first[:, 128 * h : 128 * h + 128]
            pxl[sh, sx, :, 0:16] = one[:64].reshape(ZL, 16, 128)
            pzl[sh, sx] = one[64:].reshape(ZL, 24, 128)
            one = third[:, 128 * h : 128 * h + 128]
            pxl[sh, sx, :, 16:40] = one[:96].reshape(ZL, 24, 128)
            py[sh, sx] = one[96:].reshape(NY, 8, 128)

    zlate = [
        remote(
            pzl.at[zs[i] // ZL, :, lax.rem(zs[i], ZL)], rzl.at[i], zsem.at[1, i], zrec.at[1, i], zdev[i]
        )
        for i in range(7)
    ]
    y1 = [remote(py.at[:, :, ys[i]], ry1.at[i], y1sem.at[i], y1rec.at[i], ydev[i]) for i in range(7)]
    xl = [
        remote(pxl.at[:, xs[i]], rxl.at[i], xsem.at[1, i], xrec.at[1, i], xdev[i]) for i in range(3)
    ]

    received(gz0)
    gx0 = [
        remote(wp.at[0, :, x], wp.at[0, :, x], gsem.at[31 + i], grec.at[31 + i], xdev[i])
        for i in range(3)
    ]
    received(gz1)
    gy1 = [
        remote(wp.at[1, :, :, :, y], wp.at[1, :, :, :, y], gsem.at[24 + i], grec.at[24 + i], ydev[i])
        for i in range(7)
    ]
    received(xe)
    for h in range(2):
        total = pxe[h, x]
        for i in range(3):
            total = total + rxe[i, h]
        sxe[h] = total
    y2 = [remote(sxe.at[:, ys[i]], ry2.at[i], y2sem.at[i], y2rec.at[i], ydev[i]) for i in range(7)]
    received(y1)
    total = py[:, :, y]
    for i in range(7):
        total = total + ry1[i]
    sy[...] = total
    x3 = [remote(sy.at[:, xs[i]], rx3.at[i], x3sem.at[i], x3rec.at[i], xdev[i]) for i in range(3)]
    received(xl)
    for h in range(2):
        total = pxl[h, x]
        for i in range(3):
            total = total + rxl[i, h]
        sxl[h] = total
    z2 = [
        remote(sxl.at[zs[i] // ZL, lax.rem(zs[i], ZL)], rz2.at[i], z2sem.at[i], z2rec.at[i], zdev[i])
        for i in range(7)
    ]
    received(ze)
    received(zlate)
    early = pze[zh, :, zl]
    late = pzl[zh, :, zl]
    for i in range(7):
        early = early + rze[i]
        late = late + rzl[i]
    sz[:, 0:8] = early
    sz[:, 8:32] = late
    x2 = [remote(sz.at[xs[i]], rx2.at[i], x2sem.at[i], x2rec.at[i], xdev[i]) for i in range(3)]

    received(gx0)
    received(gy1)
    local[4].wait()
    for pr in range(4):
        cols = []
        for sidx in (2 * pr, 2 * pr + 1):
            halves = [
                wp[half, sidx // NX, sidx % NX].astype(F32).reshape(32, 8, 128) for half in range(2)
            ]
            cols.append(jnp.concatenate(halves, axis=1).reshape(512, 128).astype(BF16))
        both = jnp.concatenate(cols, axis=1)
        wmat[:, 256 * pr : 256 * pr + 256] = fdot(spr[...], both).astype(BF16)

    def image(img, put):
        for h in range(0, ROWS, 2):
            total = None
            for j in range(3):
                base = (img * 8 + h + 2 - j) * WIDTH
                term = fdot(wmat[HALF * j : HALF * j + HALF, :], q[:, base : base + 256])
                total = term if total is None else total + term
            total = total.astype(BF16)
            put(h, total[:, :WIDTH])
            put(h + 1, total[:, WIDTH:])

    mine = pl.ds(pl.multiple_of(core * HALF, HALF), HALF)

    def put_peer(h, v):
        igs[h] = v

    def put_own(h, v):
        igr[h, mine, :] = v

    image(1, put_peer)
    back = remote(igs, igr.at[:, mine], isem, irec, pair)

    received(y2)
    total = sxe[:, y]
    for i in range(7):
        total = total + ry2[i]
    tz[:, 0:16] = total
    received(x3)
    total = sy[:, x]
    for i in range(3):
        total = total + rx3[i]
    tz[:, 16:24] = total
    for h in range(2):
        for v in range(ZL):
            for k in range(6):
                tzr[h, v, k : k + 1, :] = tz[h, ZL * k + v : ZL * k + v + 1, :]
    z3 = [
        remote(tzr.at[zs[i] // ZL, lax.rem(zs[i], ZL)], rz3.at[i], z3sem.at[i], z3rec.at[i], zdev[i])
        for i in range(7)
    ]
    received(z2)
    total = sxl[zh, zl]
    for i in range(7):
        total = total + rz2[i]
    ty[0:40] = total
    received(x2)
    total = sz[x]
    for i in range(3):
        total = total + rx2[i]
    ty[40:72] = total
    for v in range(NY):
        for k in range(9):
            tyr[v, k : k + 1, :] = ty[NY * k + v : NY * k + v + 1, :]
    y3 = [remote(tyr.at[ys[i]], ry3.at[i], y3sem.at[i], y3rec.at[i], ydev[i]) for i in range(7)]

    image(0, put_own)
    local[3].wait()
    back.wait_recv()
    for h in range(0, ROWS, 2):
        both = jnp.concatenate([igr[h], igr[h + 1]], axis=1)
        out = fdot(permt[...], both).astype(BF16)
        ig_ref[h] = out[:, :WIDTH]
        ig_ref[h + 1] = out[:, WIDTH:]

    received(z3)
    total = tzr[zh, zl]
    for i in range(7):
        total = total + rz3[i]
    total = total * scale
    kg_ref[1, 0:4] = total[0:4]
    kg_ref[2, 3:5] = total[4:6]
    received(y3)
    total = tyr[y]
    for i in range(7):
        total = total + ry3[i]
    total = total * scale
    kg_ref[0, 0:2] = total[0:2]
    kg_ref[2, 0:3] = total[2:5]
    kg_ref[1, 4:5] = total[5:6]
    kg_ref[0, 2:5] = total[6:9]
    for c in sent:
        c.wait_send()

    @pl.when(outer)
    def _():
        for c in halo_down:
            c.wait_send()

    @pl.when(inner)
    def _():
        for c in halo_up:
            c.wait_send()


def body(activations, out_grad, weights):
    cells = 64 * 48 * 128
    scale = 1.0 / math.sqrt(cells)
    act = jnp.transpose(activations[0], (1, 0, 2))
    grad = jnp.transpose(out_grad[0], (1, 0, 2))
    piece = jnp.transpose(weights.reshape(KI, 3, 3, KO), (1, 0, 2, 3)).reshape(3 * KI, 3 * KO)
    piece = jnp.pad(piece, ((0, 1), (0, 8))).reshape(2, 8, 128)
    gather, perm = permutation()
    hbm = pl.BlockSpec(memory_space=pltpu.HBM)
    vmem = pl.BlockSpec(memory_space=pltpu.VMEM)
    V = pltpu.VMEM
    D = pltpu.SemaphoreType.DMA

    def run(*args):
        kernel(scale, *args)

    ig, kg = pl.pallas_call(
        run,
        out_shape=(
            jax.ShapeDtypeStruct((ROWS, CH, WIDTH), BF16),
            jax.ShapeDtypeStruct((3, 8, 128), F32),
        ),
        in_specs=[hbm, hbm, vmem, hbm, hbm, hbm],
        out_specs=(vmem, vmem),
        scratch_shapes=[
            V((2, ROWS, CH, WIDTH), BF16),
            V((2, 8, CH, WIDTH), BF16),
            V((3 * HALF, CH), BF16),
            V((CH, CH), BF16),
            V((3 * HALF, 512), BF16),
            V((3 * HALF, 2 * ROWS * WIDTH), BF16),
            V((1024, 2048), BF16),
            V((2, 2, NX, ZL, NY, 8, 128), BF16),
            V((3 * HALF, 1024), BF16),
            V((ROWS, HALF, WIDTH), BF16),
            V((ROWS, CH, WIDTH), BF16),
            V((2, NX, NY, 16, 128), F32),
            V((2, NX, ZL, 40, 128), F32),
            V((2, NX, ZL, 8, 128), F32),
            V((2, NX, ZL, 24, 128), F32),
            V((2, NX, NY, 8, 128), F32),
            V((3, 2, NY, 16, 128), F32),
            V((3, 2, ZL, 40, 128), F32),
            V((7, NX, 8, 128), F32),
            V((7, NX, 24, 128), F32),
            V((7, 2, NX, 8, 128), F32),
            V((2, NY, 16, 128), F32),
            V((2, ZL, 40, 128), F32),
            V((NX, 32, 128), F32),
            V((2, NX, 8, 128), F32),
            V((7, 2, 16, 128), F32),
            V((7, 40, 128), F32),
            V((3, 32, 128), F32),
            V((3, 2, 8, 128), F32),
            V((72, 128), F32),
            V((NY, 16, 128), F32),
            V((7, 16, 128), F32),
            V((2, 24, 128), F32),
            V((2, ZL, 8, 128), F32),
            V((7, 8, 128), F32),
            D((7,)), D((2,)), D((2,)), D((2, 4)), D((2, 4)), D((2, 4)), D((2, 4)), D((34,)), D((34,)),
            D((2, 3)), D((2, 3)), D((2, 7)), D((2, 7)), D((7,)), D((7,)), D((7,)), D((7,)), D((7,)), D((7,)),
            D((3,)), D((3,)), D((3,)), D((3,)), D((7,)), D((7,)), D((7,)), D((7,)), D(()), D(()),
        ],
        compiler_params=pltpu.CompilerParams(
            collective_id=0, has_side_effects=True, vmem_limit_bytes=60 << 20
        ),
    )(
        act, grad, piece,
        jnp.asarray(gather, BF16), jnp.asarray(perm, BF16), jnp.asarray(spread(), BF16),
    )
    input_grad = jnp.transpose(ig, (1, 0, 2))[None]
    kg = kg[:, :KI, : 3 * KO].reshape(3, KI, 3, KO)
    kernel_grad = jnp.transpose(kg, (1, 0, 2, 3)).reshape(KI, 9, KO)
    return input_grad, kernel_grad


def solution(mesh):
    in_specs = (
        P("band", None, "strip", None),
        P("band", None, "strip", None),
        P("band", None, "strip"),
    )
    out_specs = (P("band", None, "strip", None), P("band", None, "strip"))
    return jax.shard_map(body, mesh=mesh, in_specs=in_specs, out_specs=out_specs, check_vma=False)
```

```python
import math

import jax
import jax.numpy as jnp
import numpy as np
from jax import lax
from jax.experimental import pallas as pl
from jax.experimental.pallas import tpu as pltpu
from jax.sharding import PartitionSpec as P

MESH = pl.DeviceIdType.MESH
BF16 = jnp.bfloat16
F32 = jnp.float32

ROWS = 6
CH = 320
WIDTH = 128
NX, NY, NZ = 4, 8, 8
ZL = 4
KI = 5
KO = 40
HALF = CH // 2
NT = (((1,), (1,)), ((), ()))


def row_order():
    rows = {0: [], 1: [], 2: []}
    for y in range(NY):
        for k in range(4):
            rows[1] += [(zl, y, k) for zl in range(ZL)]
    for zl in range(ZL):
        rows[1] += [(zl, y, 4) for y in range(NY)]
    for ks in ((0, 1), (2, 3, 4)):
        for zl in range(ZL):
            for k in ks:
                rows[0] += [(zl, y, k) for y in range(NY)]
    for zl in range(ZL):
        for k in (0, 1, 2):
            rows[2] += [(zl, y, k) for y in range(NY)]
    for y in range(NY):
        for k in (3, 4):
            rows[2] += [(zl, y, k) for zl in range(ZL)]
    return rows[0] + rows[1] + rows[2]


def permutation():
    perm = np.zeros((CH, CH), np.float32)
    gather = np.zeros((2, 3 * HALF, CH), np.float32)
    for core in range(2):
        for m in range(HALF):
            perm[2 * KI * (m // KI) + KI * core + m % KI, core * HALF + m] = 1.0
        for m, (zl, y, k) in enumerate(row_order()):
            gather[core, m, 2 * KI * (zl * NY + y) + KI * core + k] = 1.0
    return gather, perm


def spread():
    out = np.zeros((3 * HALF, 32 * 16), np.float32)
    for j in range(3):
        for m in range(HALF):
            out[j * HALF + m, 16 * (m // KI) + j * KI + m % KI] = 1.0
    return out


def fdot(a, b, dims=(((1,), (0,)), ((), ()))):
    return lax.dot_general(a, b, dims, preferred_element_type=F32)


def kernel(
    scale, act_hbm, grad_hbm, taps_ref, gather_hbm, permt_hbm, spread_hbm,
    ig_ref, kg_ref,
    piece_ref, act, gext, gather, permt, spr, amat, q, wp, wmat, igs, igr,
    pxe, pxl, pze, pzl, py, rxe, rxl, rze, rzl, ry1,
    sxe, sxl, sz, sy, ry2, rz2, rx2, rx3, ty, tyr, ry3, tz, tzr, rz3,
    lsem, psem, prec, hsem, hrec, fsem, frec, gsem, grec, xsem, xrec, zsem, zrec, y1sem, y1rec,
    y2sem, y2rec, z2sem, z2rec, x2sem, x2rec, x3sem, x3rec, y3sem, y3rec, z3sem, z3rec, isem, irec,
):
    band = lax.axis_index("band")
    strip = lax.axis_index("strip")
    core = lax.rem(band, 2)
    y = lax.rem(band // 2, NY)
    zl = band // (2 * NY)
    x = lax.rem(strip, NX)
    zh = strip // NX
    z = zh * ZL + zl

    def at(zz, yy, xx):
        zzh, zzl = zz // ZL, lax.rem(zz, ZL)
        return ((zzl * NY + yy) * 2 + core, zzh * NX + xx)

    pair = (band + 1 - 2 * core, strip)
    down = (band, lax.rem(strip + 1, 8))
    up = (band, lax.rem(strip + 7, 8))
    xs = [lax.rem(x + d, NX) for d in range(1, NX)]
    ys = [lax.rem(y + d, NY) for d in range(1, NY)]
    zs = [lax.rem(z + d, NZ) for d in range(1, NZ)]
    xdev = [at(z, y, v) for v in xs]
    ydev = [at(z, v, x) for v in ys]
    zdev = [at(v, y, x) for v in zs]

    barrier = pltpu.get_barrier_semaphore()
    partners = [pair, down, up] + xdev + ydev + zdev
    for dev in partners:
        pl.semaphore_signal(barrier, inc=1, device_id=dev, device_id_type=MESH)

    local = [
        pltpu.make_async_copy(grad_hbm, gext.at[0, pl.ds(1, ROWS)], lsem.at[1]),
        pltpu.make_async_copy(act_hbm, act.at[0], lsem.at[0]),
        pltpu.make_async_copy(gather_hbm.at[core], gather, lsem.at[2]),
        pltpu.make_async_copy(permt_hbm, permt, lsem.at[3]),
        pltpu.make_async_copy(spread_hbm, spr, lsem.at[4]),
    ]
    for c in local:
        c.start()
    rows = []
    for j in range(3):
        cols = [taps_ref[3 * j + c].astype(F32) for c in range(3)]
        rows.append(jnp.concatenate(cols + [jnp.zeros((KI, 8), F32)], axis=1))
    block = jnp.concatenate(rows + [jnp.zeros((1, 128), F32)], axis=0).reshape(2, 8, 128)
    piece_ref[...] = block.astype(BF16)
    wp[:, zh, x, zl, y] = block.astype(BF16)
    tyr[...] = jnp.zeros_like(tyr)
    tzr[...] = jnp.zeros_like(tzr)

    sent = []

    def remote(src, dst, ss, rs, dev):
        c = pltpu.make_async_remote_copy(
            src_ref=src, dst_ref=dst, send_sem=ss, recv_sem=rs, device_id=dev, device_id_type=MESH
        )
        c.start()
        sent.append(c)
        return c

    def received(copies):
        for c in copies:
            c.wait_recv()

    pl.semaphore_wait(barrier, len(partners))
    inner, outer = strip > 0, strip < 7
    halo_down = []
    halo_up = []
    for n in range(4):
        part = pl.ds(80 * n, 80)
        halo_down.append(
            pltpu.make_async_remote_copy(
                src_ref=grad_hbm.at[ROWS - 1, part], dst_ref=gext.at[0, 0, part],
                send_sem=hsem.at[0, n], recv_sem=hrec.at[0, n], device_id=down, device_id_type=MESH,
            )
        )
        halo_up.append(
            pltpu.make_async_remote_copy(
                src_ref=grad_hbm.at[0, part], dst_ref=gext.at[0, ROWS + 1, part],
                send_sem=hsem.at[1, n], recv_sem=hrec.at[1, n], device_id=up, device_id_type=MESH,
            )
        )

    @pl.when(outer)
    def _():
        for c in halo_down:
            c.start()

    @pl.when(inner)
    def _():
        for c in halo_up:
            c.start()

    here = (zh, x, zl, y)
    gx = [
        remote(piece_ref.at[1], wp.at[(1, *here)], gsem.at[i], grec.at[i], xdev[i])
        for i in range(3)
    ]
    gy = [
        remote(piece_ref.at[0], wp.at[(0, *here)], gsem.at[3 + i], grec.at[3 + i], ydev[i])
        for i in (3, 2, 4, 1, 5, 0, 6)
    ]
    swap = [
        remote(grad_hbm, gext.at[1, pl.ds(1, ROWS)], psem.at[0], prec.at[0], pair),
        remote(act_hbm, act.at[1], psem.at[1], prec.at[1], pair),
    ]

    lane = lax.broadcasted_iota(jnp.int32, (80, WIDTH), 1)
    zero8 = jnp.zeros((8, WIDTH), F32)

    def fill(img, e, keep=None, parts=range(4)):
        col = pl.ds(pl.multiple_of((img * 8 + e) * WIDTH, WIDTH), WIDTH)
        for pr in parts:
            g = gext[img, e, 80 * pr : 80 * pr + 80, :].astype(F32)
            if keep is not None:
                g = jnp.where(keep, g, 0.0)
            nxt = jnp.where(lane == WIDTH - 1, 0.0, pltpu.roll(g, WIDTH - 1, 1))
            prv = jnp.where(lane == 0, 0.0, pltpu.roll(g, 1, 1))
            for h in range(2):
                sl = slice(40 * h, 40 * h + 40)
                block = jnp.concatenate([nxt[sl], g[sl], prv[sl], zero8], axis=0)
                base = (2 * pr + h) * 128
                q[base : base + 128, col] = block.astype(BF16)

    def fill_image(img):
        @pl.loop(1, ROWS + 1)
        def _(e):
            fill(img, e)

    def rows_image(img):
        for h in range(0, ROWS, 2):
            both = jnp.concatenate([act[img, h], act[img, h + 1]], axis=1)
            base = img * ROWS * WIDTH + h * WIDTH
            amat[:, base : base + 2 * WIDTH] = fdot(gather[...], both).astype(BF16)

    def forward(n):
        part = pl.ds(80 * n, 80)

        @pl.when(inner)
        def _():
            halo_down[n].wait_recv()

        @pl.when(outer)
        def _():
            halo_up[n].wait_recv()

        return [
            remote(gext.at[0, e, part], gext.at[1, e, part], fsem.at[i, n], frec.at[i, n], pair)
            for i, e in enumerate((0, ROWS + 1))
        ]

    local[0].wait()
    fill_image(0)
    local[1].wait()
    local[2].wait()
    rows_image(0)
    swap[0].wait_recv()
    fill_image(1)
    swap[1].wait_recv()
    rows_image(1)
    span = ROWS * WIDTH

    def product(j, n):
        rows = pl.ds(256 * n if isinstance(n, int) else pl.multiple_of(n * 256, 256), 256)
        mine = slice(HALF * j, HALF * j + HALF)
        total = fdot(amat[mine, 0:span], q[rows, (2 - j) * WIDTH : (2 - j) * WIDTH + span], NT)
        return total + fdot(
            amat[mine, span : 2 * span], q[rows, (10 - j) * WIDTH : (10 - j) * WIDTH + span], NT
        )

    @pl.loop(0, 4)
    def _(n):
        total = product(1, n)
        for h in range(2):
            sh, sx = n // 2, 2 * lax.rem(n, 2) + h
            one = total[:, 128 * h : 128 * h + 128]
            pxe[sh, sx] = one[:128].reshape(NY, 16, 128)
            pze[sh, sx] = one[128:].reshape(ZL, 8, 128)

    xe = [
        remote(pxe.at[:, xs[i]], rxe.at[i], xsem.at[0, i], xrec.at[0, i], xdev[i]) for i in range(3)
    ]
    ze = [
        remote(
            pze.at[zs[i] // ZL, :, lax.rem(zs[i], ZL)], rze.at[i], zsem.at[0, i], zrec.at[0, i], zdev[i]
        )
        for i in (3, 2, 4, 1, 5, 0, 6)
    ]

    received(gx)
    gz1 = [
        remote(wp.at[1, zh, :, zl, y], wp.at[1, zh, :, zl, y], gsem.at[10 + i], grec.at[10 + i], zdev[i])
        for i in (3, 2, 4, 1, 5, 0, 6)
    ]
    received(gy)
    gz0 = [
        remote(wp.at[0, zh, x, zl], wp.at[0, zh, x, zl], gsem.at[17 + i], grec.at[17 + i], zdev[i])
        for i in (3, 2, 4, 1, 5, 0, 6)
    ]
    ahead = forward(0)
    for n in range(4):
        now = ahead
        if n < 3:
            ahead = forward(n + 1)
        fill(0, 0, inner, (n,))
        fill(0, ROWS + 1, outer, (n,))
        now[0].wait_recv()
        fill(1, 0, inner, (n,))
        now[1].wait_recv()
        fill(1, ROWS + 1, outer, (n,))
        first = product(0, n)
        third = product(2, n)
        for h in range(2):
            sh, sx = n // 2, 2 * (n % 2) + h
            one = first[:, 128 * h : 128 * h + 128]
            pxl[sh, sx, :, 0:16] = one[:64].reshape(ZL, 16, 128)
            pzl[sh, sx] = one[64:].reshape(ZL, 24, 128)
            one = third[:, 128 * h : 128 * h + 128]
            pxl[sh, sx, :, 16:40] = one[:96].reshape(ZL, 24, 128)
            py[sh, sx] = one[96:].reshape(NY, 8, 128)

    zlate = [
        remote(
            pzl.at[zs[i] // ZL, :, lax.rem(zs[i], ZL)], rzl.at[i], zsem.at[1, i], zrec.at[1, i], zdev[i]
        )
        for i in (3, 2, 4, 1, 5, 0, 6)
    ]
    y1 = [remote(py.at[:, :, ys[i]], ry1.at[i], y1sem.at[i], y1rec.at[i], ydev[i]) for i in (3, 2, 4, 1, 5, 0, 6)]
    xl = [
        remote(pxl.at[:, xs[i]], rxl.at[i], xsem.at[1, i], xrec.at[1, i], xdev[i]) for i in range(3)
    ]

    received(gz0)
    gx0 = [
        remote(wp.at[0, :, x], wp.at[0, :, x], gsem.at[31 + i], grec.at[31 + i], xdev[i])
        for i in range(3)
    ]
    received(gz1)
    gy1 = [
        remote(wp.at[1, :, :, :, y], wp.at[1, :, :, :, y], gsem.at[24 + i], grec.at[24 + i], ydev[i])
        for i in (3, 2, 4, 1, 5, 0, 6)
    ]
    received(xe)
    for h in range(2):
        total = pxe[h, x]
        for i in range(3):
            total = total + rxe[i, h]
        sxe[h] = total
    y2 = [remote(sxe.at[:, ys[i]], ry2.at[i], y2sem.at[i], y2rec.at[i], ydev[i]) for i in (3, 2, 4, 1, 5, 0, 6)]
    received(y1)
    total = py[:, :, y]
    for i in range(7):
        total = total + ry1[i]
    sy[...] = total
    x3 = [remote(sy.at[:, xs[i]], rx3.at[i], x3sem.at[i], x3rec.at[i], xdev[i]) for i in range(3)]
    received(xl)
    for h in range(2):
        total = pxl[h, x]
        for i in range(3):
            total = total + rxl[i, h]
        sxl[h] = total
    z2 = [
        remote(sxl.at[zs[i] // ZL, lax.rem(zs[i], ZL)], rz2.at[i], z2sem.at[i], z2rec.at[i], zdev[i])
        for i in (3, 2, 4, 1, 5, 0, 6)
    ]
    received(ze)
    received(zlate)
    early = pze[zh, :, zl]
    late = pzl[zh, :, zl]
    for i in range(7):
        early = early + rze[i]
        late = late + rzl[i]
    sz[:, 0:8] = early
    sz[:, 8:32] = late
    x2 = [remote(sz.at[xs[i]], rx2.at[i], x2sem.at[i], x2rec.at[i], xdev[i]) for i in range(3)]

    received(gx0)
    received(gy1)
    local[4].wait()
    for pr in range(4):
        cols = []
        for sidx in (2 * pr, 2 * pr + 1):
            halves = [
                wp[half, sidx // NX, sidx % NX].astype(F32).reshape(32, 8, 128) for half in range(2)
            ]
            cols.append(jnp.concatenate(halves, axis=1).reshape(512, 128).astype(BF16))
        both = jnp.concatenate(cols, axis=1)
        wmat[:, 256 * pr : 256 * pr + 256] = fdot(spr[...], both).astype(BF16)

    def image(img, put):
        for h in range(0, ROWS, 2):
            total = None
            for j in range(3):
                base = (img * 8 + h + 2 - j) * WIDTH
                term = fdot(wmat[HALF * j : HALF * j + HALF, :], q[:, base : base + 256])
                total = term if total is None else total + term
            total = total.astype(BF16)
            put(h, total[:, :WIDTH])
            put(h + 1, total[:, WIDTH:])

    mine = pl.ds(pl.multiple_of(core * HALF, HALF), HALF)

    def put_peer(h, v):
        igs[h] = v

    def put_own(h, v):
        igr[h, mine, :] = v

    image(1, put_peer)
    back = remote(igs, igr.at[:, mine], isem, irec, pair)

    received(y2)
    total = sxe[:, y]
    for i in range(7):
        total = total + ry2[i]
    tz[:, 0:16] = total
    received(x3)
    total = sy[:, x]
    for i in range(3):
        total = total + rx3[i]
    tz[:, 16:24] = total
    for h in range(2):
        for v in range(ZL):
            for k in range(6):
                tzr[h, v, k : k + 1, :] = tz[h, ZL * k + v : ZL * k + v + 1, :]
    z3 = [
        remote(tzr.at[zs[i] // ZL, lax.rem(zs[i], ZL)], rz3.at[i], z3sem.at[i], z3rec.at[i], zdev[i])
        for i in (3, 2, 4, 1, 5, 0, 6)
    ]
    received(z2)
    total = sxl[zh, zl]
    for i in range(7):
        total = total + rz2[i]
    ty[0:40] = total
    received(x2)
    total = sz[x]
    for i in range(3):
        total = total + rx2[i]
    ty[40:72] = total
    for v in range(NY):
        for k in range(9):
            tyr[v, k : k + 1, :] = ty[NY * k + v : NY * k + v + 1, :]
    y3 = [remote(tyr.at[ys[i]], ry3.at[i], y3sem.at[i], y3rec.at[i], ydev[i]) for i in (3, 2, 4, 1, 5, 0, 6)]

    image(0, put_own)
    local[3].wait()
    back.wait_recv()
    for h in range(0, ROWS, 2):
        both = jnp.concatenate([igr[h], igr[h + 1]], axis=1)
        out = fdot(permt[...], both).astype(BF16)
        ig_ref[h] = out[:, :WIDTH]
        ig_ref[h + 1] = out[:, WIDTH:]

    received(z3)
    total = tzr[zh, zl]
    for i in range(7):
        total = total + rz3[i]
    total = total * scale

    def put(j, k0, rows):
        for c in range(3):
            kg_ref[3 * j + c, k0 : k0 + rows.shape[0], :] = rows[:, 40 * c : 40 * c + 40]

    put(1, 0, total[0:4])
    put(2, 3, total[4:6])
    received(y3)
    total = tyr[y]
    for i in range(7):
        total = total + ry3[i]
    total = total * scale
    put(0, 0, total[0:2])
    put(2, 0, total[2:5])
    put(1, 4, total[5:6])
    put(0, 2, total[6:9])
    for c in sent:
        c.wait_send()

    @pl.when(outer)
    def _():
        for c in halo_down:
            c.wait_send()

    @pl.when(inner)
    def _():
        for c in halo_up:
            c.wait_send()


def body(activations, out_grad, weights):
    cells = 64 * 48 * 128
    scale = 1.0 / math.sqrt(cells)
    act = jnp.transpose(activations[0], (1, 0, 2))
    grad = jnp.transpose(out_grad[0], (1, 0, 2))
    piece = jnp.transpose(weights, (1, 0, 2))
    gather, perm = permutation()
    hbm = pl.BlockSpec(memory_space=pltpu.HBM)
    vmem = pl.BlockSpec(memory_space=pltpu.VMEM)
    V = pltpu.VMEM
    D = pltpu.SemaphoreType.DMA

    def run(*args):
        kernel(scale, *args)

    ig, kg = pl.pallas_call(
        run,
        out_shape=(
            jax.ShapeDtypeStruct((ROWS, CH, WIDTH), BF16),
            jax.ShapeDtypeStruct((9, KI, KO), F32),
        ),
        in_specs=[hbm, hbm, vmem, hbm, hbm, hbm],
        out_specs=(vmem, vmem),
        scratch_shapes=[
            V((2, 8, 128), BF16),
            V((2, ROWS, CH, WIDTH), BF16),
            V((2, 8, CH, WIDTH), BF16),
            V((3 * HALF, CH), BF16),
            V((CH, CH), BF16),
            V((3 * HALF, 512), BF16),
            V((3 * HALF, 2 * ROWS * WIDTH), BF16),
            V((1024, 2048), BF16),
            V((2, 2, NX, ZL, NY, 8, 128), BF16),
            V((3 * HALF, 1024), BF16),
            V((ROWS, HALF, WIDTH), BF16),
            V((ROWS, CH, WIDTH), BF16),
            V((2, NX, NY, 16, 128), F32),
            V((2, NX, ZL, 40, 128), F32),
            V((2, NX, ZL, 8, 128), F32),
            V((2, NX, ZL, 24, 128), F32),
            V((2, NX, NY, 8, 128), F32),
            V((3, 2, NY, 16, 128), F32),
            V((3, 2, ZL, 40, 128), F32),
            V((7, NX, 8, 128), F32),
            V((7, NX, 24, 128), F32),
            V((7, 2, NX, 8, 128), F32),
            V((2, NY, 16, 128), F32),
            V((2, ZL, 40, 128), F32),
            V((NX, 32, 128), F32),
            V((2, NX, 8, 128), F32),
            V((7, 2, 16, 128), F32),
            V((7, 40, 128), F32),
            V((3, 32, 128), F32),
            V((3, 2, 8, 128), F32),
            V((72, 128), F32),
            V((NY, 16, 128), F32),
            V((7, 16, 128), F32),
            V((2, 24, 128), F32),
            V((2, ZL, 8, 128), F32),
            V((7, 8, 128), F32),
            D((5,)), D((2,)), D((2,)), D((2, 4)), D((2, 4)), D((2, 4)), D((2, 4)), D((34,)), D((34,)),
            D((2, 3)), D((2, 3)), D((2, 7)), D((2, 7)), D((7,)), D((7,)), D((7,)), D((7,)), D((7,)), D((7,)),
            D((3,)), D((3,)), D((3,)), D((3,)), D((7,)), D((7,)), D((7,)), D((7,)), D(()), D(()),
        ],
        compiler_params=pltpu.CompilerParams(
            collective_id=0, has_side_effects=True, vmem_limit_bytes=60 << 20
        ),
    )(
        act, grad, piece,
        jnp.asarray(gather, BF16), jnp.asarray(perm, BF16), jnp.asarray(spread(), BF16),
    )
    input_grad = jnp.transpose(ig, (1, 0, 2))[None]
    kernel_grad = jnp.transpose(kg, (1, 0, 2))
    return input_grad, kernel_grad


def solution(mesh):
    in_specs = (
        P("band", None, "strip", None),
        P("band", None, "strip", None),
        P("band", None, "strip"),
    )
    out_specs = (P("band", None, "strip", None), P("band", None, "strip"))
    return jax.shard_map(body, mesh=mesh, in_specs=in_specs, out_specs=out_specs, check_vma=False)
```

```python
import math

import jax
import jax.numpy as jnp
import numpy as np
from jax import lax
from jax.experimental import pallas as pl
from jax.experimental.pallas import tpu as pltpu
from jax.sharding import PartitionSpec as P

MESH = pl.DeviceIdType.MESH
BF16 = jnp.bfloat16
F32 = jnp.float32

ROWS = 6
CH = 320
WIDTH = 128
NX, NY, NZ = 4, 8, 8
ZL = 4
KI = 5
KO = 40
HALF = CH // 2
NT = (((1,), (1,)), ((), ()))


def row_order():
    rows = {0: [], 1: [], 2: []}
    for y in range(NY):
        for k in range(4):
            rows[1] += [(zl, y, k) for zl in range(ZL)]
    for zl in range(ZL):
        rows[1] += [(zl, y, 4) for y in range(NY)]
    for ks in ((0, 1), (2, 3, 4)):
        for zl in range(ZL):
            for k in ks:
                rows[0] += [(zl, y, k) for y in range(NY)]
    for zl in range(ZL):
        for k in (0, 1, 2):
            rows[2] += [(zl, y, k) for y in range(NY)]
    for y in range(NY):
        for k in (3, 4):
            rows[2] += [(zl, y, k) for zl in range(ZL)]
    return rows[0] + rows[1] + rows[2]


def permutation():
    perm = np.zeros((CH, CH), np.float32)
    gather = np.zeros((2, 3 * HALF, CH), np.float32)
    for core in range(2):
        for m in range(HALF):
            perm[2 * KI * (m // KI) + KI * core + m % KI, core * HALF + m] = 1.0
        for m, (zl, y, k) in enumerate(row_order()):
            gather[core, m, 2 * KI * (zl * NY + y) + KI * core + k] = 1.0
    return gather, perm


def spread():
    out = np.zeros((3 * HALF, 32 * 16), np.float32)
    for j in range(3):
        for m in range(HALF):
            out[j * HALF + m, 16 * (m // KI) + j * KI + m % KI] = 1.0
    return out


def fdot(a, b, dims=(((1,), (0,)), ((), ()))):
    return lax.dot_general(a, b, dims, preferred_element_type=F32)


def kernel(
    scale, act_hbm, grad_hbm, taps_ref, gather_hbm, permt_hbm, spread_hbm,
    ig_ref, kg_ref,
    piece_ref, act, gext, gather, permt, spr, amat, q, wp, wmat, igs, igr,
    pxe, pxl, pze, pzl, py, rxe, rxl, rze, rzl, ry1,
    sxe, sxl, sz, sy, ry2, rz2, rx2, rx3, ty, tyr, ry3, tz, tzr, rz3,
    lsem, psem, prec, hsem, hrec, fsem, frec, gsem, grec, xsem, xrec, zsem, zrec, y1sem, y1rec,
    y2sem, y2rec, z2sem, z2rec, x2sem, x2rec, x3sem, x3rec, y3sem, y3rec, z3sem, z3rec, isem, irec,
):
    band = lax.axis_index("band")
    strip = lax.axis_index("strip")
    core = lax.rem(band, 2)
    y = lax.rem(band // 2, NY)
    zl = band // (2 * NY)
    x = lax.rem(strip, NX)
    zh = strip // NX
    z = zh * ZL + zl

    def at(zz, yy, xx):
        zzh, zzl = zz // ZL, lax.rem(zz, ZL)
        return ((zzl * NY + yy) * 2 + core, zzh * NX + xx)

    pair = (band + 1 - 2 * core, strip)
    down = (band, lax.rem(strip + 1, 8))
    up = (band, lax.rem(strip + 7, 8))
    xs = [lax.rem(x + d, NX) for d in range(1, NX)]
    ys = [lax.rem(y + d, NY) for d in range(1, NY)]
    zs = [lax.rem(z + d, NZ) for d in range(1, NZ)]
    xdev = [at(z, y, v) for v in xs]
    ydev = [at(z, v, x) for v in ys]
    zdev = [at(v, y, x) for v in zs]

    barrier = pltpu.get_barrier_semaphore()
    partners = [pair, down, up] + xdev + ydev + zdev
    for dev in partners:
        pl.semaphore_signal(barrier, inc=1, device_id=dev, device_id_type=MESH)

    local = [
        pltpu.make_async_copy(grad_hbm, gext.at[0, pl.ds(1, ROWS)], lsem.at[1]),
        pltpu.make_async_copy(act_hbm, act.at[0], lsem.at[0]),
        pltpu.make_async_copy(gather_hbm.at[core], gather, lsem.at[2]),
        pltpu.make_async_copy(permt_hbm, permt, lsem.at[3]),
        pltpu.make_async_copy(spread_hbm, spr, lsem.at[4]),
    ]
    for c in local:
        c.start()
    rows = []
    for j in range(3):
        cols = [taps_ref[3 * j + c].astype(F32) for c in range(3)]
        rows.append(jnp.concatenate(cols + [jnp.zeros((KI, 8), F32)], axis=1))
    block = jnp.concatenate(rows + [jnp.zeros((1, 128), F32)], axis=0).reshape(2, 8, 128)
    piece_ref[...] = block.astype(BF16)
    wp[:, zh, x, zl, y] = block.astype(BF16)
    tyr[...] = jnp.zeros_like(tyr)
    tzr[...] = jnp.zeros_like(tzr)

    sent = []

    def remote(src, dst, ss, rs, dev):
        c = pltpu.make_async_remote_copy(
            src_ref=src, dst_ref=dst, send_sem=ss, recv_sem=rs, device_id=dev, device_id_type=MESH
        )
        c.start()
        sent.append(c)
        return c

    def received(copies):
        for c in copies:
            c.wait_recv()

    pl.semaphore_wait(barrier, len(partners))
    inner, outer = strip > 0, strip < 7
    halo_down = []
    halo_up = []
    for n in range(4):
        part = pl.ds(80 * n, 80)
        halo_down.append(
            pltpu.make_async_remote_copy(
                src_ref=grad_hbm.at[ROWS - 1, part], dst_ref=gext.at[0, 0, part],
                send_sem=hsem.at[0, n], recv_sem=hrec.at[0, n], device_id=down, device_id_type=MESH,
            )
        )
        halo_up.append(
            pltpu.make_async_remote_copy(
                src_ref=grad_hbm.at[0, part], dst_ref=gext.at[0, ROWS + 1, part],
                send_sem=hsem.at[1, n], recv_sem=hrec.at[1, n], device_id=up, device_id_type=MESH,
            )
        )

    @pl.when(outer)
    def _():
        for c in halo_down:
            c.start()

    @pl.when(inner)
    def _():
        for c in halo_up:
            c.start()

    here = (zh, x, zl, y)
    gx = [
        remote(piece_ref.at[1], wp.at[(1, *here)], gsem.at[i], grec.at[i], xdev[i])
        for i in range(3)
    ]
    gy = [
        remote(piece_ref.at[0], wp.at[(0, *here)], gsem.at[3 + i], grec.at[3 + i], ydev[i])
        for i in (3, 2, 4, 1, 5, 0, 6)
    ]
    swap = [
        remote(grad_hbm, gext.at[1, pl.ds(1, ROWS)], psem.at[0], prec.at[0], pair),
        remote(act_hbm, act.at[1], psem.at[1], prec.at[1], pair),
    ]

    lane = lax.broadcasted_iota(jnp.int32, (80, WIDTH), 1)
    zero8 = jnp.zeros((8, WIDTH), F32)

    def fill(img, e, keep=None, parts=range(4)):
        col = pl.ds(pl.multiple_of((img * 8 + e) * WIDTH, WIDTH), WIDTH)
        for pr in parts:
            g = gext[img, e, 80 * pr : 80 * pr + 80, :].astype(F32)
            if keep is not None:
                g = jnp.where(keep, g, 0.0)
            nxt = jnp.where(lane == WIDTH - 1, 0.0, pltpu.roll(g, WIDTH - 1, 1))
            prv = jnp.where(lane == 0, 0.0, pltpu.roll(g, 1, 1))
            for h in range(2):
                sl = slice(40 * h, 40 * h + 40)
                block = jnp.concatenate([nxt[sl], g[sl], prv[sl], zero8], axis=0)
                base = (2 * pr + h) * 128
                q[base : base + 128, col] = block.astype(BF16)

    def fill_image(img):
        @pl.loop(1, ROWS + 1)
        def _(e):
            fill(img, e)

    def rows_image(img):
        for h in range(0, ROWS, 2):
            both = jnp.concatenate([act[img, h], act[img, h + 1]], axis=1)
            base = img * ROWS * WIDTH + h * WIDTH
            amat[:, base : base + 2 * WIDTH] = fdot(gather[...], both).astype(BF16)

    def forward(n):
        part = pl.ds(80 * n, 80)

        @pl.when(inner)
        def _():
            halo_down[n].wait_recv()

        @pl.when(outer)
        def _():
            halo_up[n].wait_recv()

        return [
            remote(gext.at[0, e, part], gext.at[1, e, part], fsem.at[i, n], frec.at[i, n], pair)
            for i, e in enumerate((0, ROWS + 1))
        ]

    local[0].wait()
    fill_image(0)
    local[1].wait()
    local[2].wait()
    rows_image(0)
    swap[0].wait_recv()
    fill_image(1)
    swap[1].wait_recv()
    rows_image(1)
    span = ROWS * WIDTH

    def product(j, n):
        rows = pl.ds(256 * n if isinstance(n, int) else pl.multiple_of(n * 256, 256), 256)
        mine = slice(HALF * j, HALF * j + HALF)
        total = fdot(amat[mine, 0:span], q[rows, (2 - j) * WIDTH : (2 - j) * WIDTH + span], NT)
        return total + fdot(
            amat[mine, span : 2 * span], q[rows, (10 - j) * WIDTH : (10 - j) * WIDTH + span], NT
        )

    @pl.loop(0, 4)
    def _(n):
        total = product(1, n)
        for h in range(2):
            sh, sx = n // 2, 2 * lax.rem(n, 2) + h
            one = total[:, 128 * h : 128 * h + 128]
            pxe[sh, sx] = one[:128].reshape(NY, 16, 128)
            pze[sh, sx] = one[128:].reshape(ZL, 8, 128)

    xe = [
        remote(pxe.at[:, xs[i]], rxe.at[i], xsem.at[0, i], xrec.at[0, i], xdev[i]) for i in range(3)
    ]
    ze = [
        remote(
            pze.at[zs[i] // ZL, :, lax.rem(zs[i], ZL)], rze.at[i], zsem.at[0, i], zrec.at[0, i], zdev[i]
        )
        for i in (3, 2, 4, 1, 5, 0, 6)
    ]

    received(gx)
    gz1 = [
        remote(wp.at[1, zh, :, zl, y], wp.at[1, zh, :, zl, y], gsem.at[10 + i], grec.at[10 + i], zdev[i])
        for i in (3, 2, 4, 1, 5, 0, 6)
    ]
    received(gy)
    gz0 = [
        remote(wp.at[0, zh, x, zl], wp.at[0, zh, x, zl], gsem.at[17 + i], grec.at[17 + i], zdev[i])
        for i in (3, 2, 4, 1, 5, 0, 6)
    ]
    ahead = forward(0)
    for n in range(4):
        now = ahead
        if n < 3:
            ahead = forward(n + 1)
        fill(0, 0, inner, (n,))
        fill(0, ROWS + 1, outer, (n,))
        now[0].wait_recv()
        fill(1, 0, inner, (n,))
        now[1].wait_recv()
        fill(1, ROWS + 1, outer, (n,))
        first = product(0, n)
        third = product(2, n)
        for h in range(2):
            sh, sx = n // 2, 2 * (n % 2) + h
            one = first[:, 128 * h : 128 * h + 128]
            pxl[sh, sx, :, 0:16] = one[:64].reshape(ZL, 16, 128)
            pzl[sh, sx] = one[64:].reshape(ZL, 24, 128)
            one = third[:, 128 * h : 128 * h + 128]
            pxl[sh, sx, :, 16:40] = one[:96].reshape(ZL, 24, 128)
            py[sh, sx] = one[96:].reshape(NY, 8, 128)

    zlate = [
        remote(
            pzl.at[zs[i] // ZL, :, lax.rem(zs[i], ZL)], rzl.at[i], zsem.at[1, i], zrec.at[1, i], zdev[i]
        )
        for i in (3, 2, 4, 1, 5, 0, 6)
    ]
    y1 = [remote(py.at[:, :, ys[i]], ry1.at[i], y1sem.at[i], y1rec.at[i], ydev[i]) for i in (3, 2, 4, 1, 5, 0, 6)]
    xl = [
        remote(pxl.at[:, xs[i]], rxl.at[i], xsem.at[1, i], xrec.at[1, i], xdev[i]) for i in range(3)
    ]

    received(gz1)
    gy1 = [
        remote(wp.at[1, :, :, :, y], wp.at[1, :, :, :, y], gsem.at[24 + i], grec.at[24 + i], ydev[i])
        for i in (3, 2, 4, 1, 5, 0, 6)
    ]
    received(gz0)
    gx0 = [
        remote(wp.at[0, :, x], wp.at[0, :, x], gsem.at[31 + i], grec.at[31 + i], xdev[i])
        for i in range(3)
    ]
    received(xe)
    for h in range(2):
        total = pxe[h, x]
        for i in range(3):
            total = total + rxe[i, h]
        sxe[h] = total
    y2 = [remote(sxe.at[:, ys[i]], ry2.at[i], y2sem.at[i], y2rec.at[i], ydev[i]) for i in (3, 2, 4, 1, 5, 0, 6)]
    received(y1)
    total = py[:, :, y]
    for i in range(7):
        total = total + ry1[i]
    sy[...] = total
    x3 = [remote(sy.at[:, xs[i]], rx3.at[i], x3sem.at[i], x3rec.at[i], xdev[i]) for i in range(3)]
    received(xl)
    for h in range(2):
        total = pxl[h, x]
        for i in range(3):
            total = total + rxl[i, h]
        sxl[h] = total
    z2 = [
        remote(sxl.at[zs[i] // ZL, lax.rem(zs[i], ZL)], rz2.at[i], z2sem.at[i], z2rec.at[i], zdev[i])
        for i in (3, 2, 4, 1, 5, 0, 6)
    ]
    received(ze)
    received(zlate)
    early = pze[zh, :, zl]
    late = pzl[zh, :, zl]
    for i in range(7):
        early = early + rze[i]
        late = late + rzl[i]
    sz[:, 0:8] = early
    sz[:, 8:32] = late
    x2 = [remote(sz.at[xs[i]], rx2.at[i], x2sem.at[i], x2rec.at[i], xdev[i]) for i in range(3)]

    received(y2)
    total = sxe[:, y]
    for i in range(7):
        total = total + ry2[i]
    tz[:, 0:16] = total
    received(x3)
    total = sy[:, x]
    for i in range(3):
        total = total + rx3[i]
    tz[:, 16:24] = total
    for h in range(2):
        for v in range(ZL):
            for k in range(6):
                tzr[h, v, k : k + 1, :] = tz[h, ZL * k + v : ZL * k + v + 1, :]
    z3 = [
        remote(tzr.at[zs[i] // ZL, lax.rem(zs[i], ZL)], rz3.at[i], z3sem.at[i], z3rec.at[i], zdev[i])
        for i in (3, 2, 4, 1, 5, 0, 6)
    ]
    received(z2)
    total = sxl[zh, zl]
    for i in range(7):
        total = total + rz2[i]
    ty[0:40] = total
    received(x2)
    total = sz[x]
    for i in range(3):
        total = total + rx2[i]
    ty[40:72] = total
    for v in range(NY):
        for k in range(9):
            tyr[v, k : k + 1, :] = ty[NY * k + v : NY * k + v + 1, :]
    y3 = [remote(tyr.at[ys[i]], ry3.at[i], y3sem.at[i], y3rec.at[i], ydev[i]) for i in (3, 2, 4, 1, 5, 0, 6)]

    received(gx0)
    received(gy1)
    local[4].wait()
    for pr in range(4):
        cols = []
        for sidx in (2 * pr, 2 * pr + 1):
            halves = [
                wp[half, sidx // NX, sidx % NX].astype(F32).reshape(32, 8, 128) for half in range(2)
            ]
            cols.append(jnp.concatenate(halves, axis=1).reshape(512, 128).astype(BF16))
        both = jnp.concatenate(cols, axis=1)
        wmat[:, 256 * pr : 256 * pr + 256] = fdot(spr[...], both).astype(BF16)

    def image(img, put):
        for h in range(0, ROWS, 2):
            total = None
            for j in range(3):
                base = (img * 8 + h + 2 - j) * WIDTH
                term = fdot(wmat[HALF * j : HALF * j + HALF, :], q[:, base : base + 256])
                total = term if total is None else total + term
            total = total.astype(BF16)
            put(h, total[:, :WIDTH])
            put(h + 1, total[:, WIDTH:])

    mine = pl.ds(pl.multiple_of(core * HALF, HALF), HALF)

    def put_peer(h, v):
        igs[h] = v

    def put_own(h, v):
        igr[h, mine, :] = v

    image(1, put_peer)
    back = remote(igs, igr.at[:, mine], isem, irec, pair)

    image(0, put_own)
    local[3].wait()
    back.wait_recv()
    for h in range(0, ROWS, 2):
        both = jnp.concatenate([igr[h], igr[h + 1]], axis=1)
        out = fdot(permt[...], both).astype(BF16)
        ig_ref[h] = out[:, :WIDTH]
        ig_ref[h + 1] = out[:, WIDTH:]

    received(z3)
    total = tzr[zh, zl]
    for i in range(7):
        total = total + rz3[i]
    total = total * scale

    def put(j, k0, rows):
        for c in range(3):
            kg_ref[3 * j + c, k0 : k0 + rows.shape[0], :] = rows[:, 40 * c : 40 * c + 40]

    put(1, 0, total[0:4])
    put(2, 3, total[4:6])
    received(y3)
    total = tyr[y]
    for i in range(7):
        total = total + ry3[i]
    total = total * scale
    put(0, 0, total[0:2])
    put(2, 0, total[2:5])
    put(1, 4, total[5:6])
    put(0, 2, total[6:9])
    for c in sent:
        c.wait_send()

    @pl.when(outer)
    def _():
        for c in halo_down:
            c.wait_send()

    @pl.when(inner)
    def _():
        for c in halo_up:
            c.wait_send()


def body(activations, out_grad, weights):
    cells = 64 * 48 * 128
    scale = 1.0 / math.sqrt(cells)
    act = jnp.transpose(activations[0], (1, 0, 2))
    grad = jnp.transpose(out_grad[0], (1, 0, 2))
    piece = jnp.transpose(weights, (1, 0, 2))
    gather, perm = permutation()
    hbm = pl.BlockSpec(memory_space=pltpu.HBM)
    vmem = pl.BlockSpec(memory_space=pltpu.VMEM)
    V = pltpu.VMEM
    D = pltpu.SemaphoreType.DMA

    def run(*args):
        kernel(scale, *args)

    ig, kg = pl.pallas_call(
        run,
        out_shape=(
            jax.ShapeDtypeStruct((ROWS, CH, WIDTH), BF16),
            jax.ShapeDtypeStruct((9, KI, KO), F32),
        ),
        in_specs=[hbm, hbm, vmem, hbm, hbm, hbm],
        out_specs=(vmem, vmem),
        scratch_shapes=[
            V((2, 8, 128), BF16),
            V((2, ROWS, CH, WIDTH), BF16),
            V((2, 8, CH, WIDTH), BF16),
            V((3 * HALF, CH), BF16),
            V((CH, CH), BF16),
            V((3 * HALF, 512), BF16),
            V((3 * HALF, 2 * ROWS * WIDTH), BF16),
            V((1024, 2048), BF16),
            V((2, 2, NX, ZL, NY, 8, 128), BF16),
            V((3 * HALF, 1024), BF16),
            V((ROWS, HALF, WIDTH), BF16),
            V((ROWS, CH, WIDTH), BF16),
            V((2, NX, NY, 16, 128), F32),
            V((2, NX, ZL, 40, 128), F32),
            V((2, NX, ZL, 8, 128), F32),
            V((2, NX, ZL, 24, 128), F32),
            V((2, NX, NY, 8, 128), F32),
            V((3, 2, NY, 16, 128), F32),
            V((3, 2, ZL, 40, 128), F32),
            V((7, NX, 8, 128), F32),
            V((7, NX, 24, 128), F32),
            V((7, 2, NX, 8, 128), F32),
            V((2, NY, 16, 128), F32),
            V((2, ZL, 40, 128), F32),
            V((NX, 32, 128), F32),
            V((2, NX, 8, 128), F32),
            V((7, 2, 16, 128), F32),
            V((7, 40, 128), F32),
            V((3, 32, 128), F32),
            V((3, 2, 8, 128), F32),
            V((72, 128), F32),
            V((NY, 16, 128), F32),
            V((7, 16, 128), F32),
            V((2, 24, 128), F32),
            V((2, ZL, 8, 128), F32),
            V((7, 8, 128), F32),
            D((5,)), D((2,)), D((2,)), D((2, 4)), D((2, 4)), D((2, 4)), D((2, 4)), D((34,)), D((34,)),
            D((2, 3)), D((2, 3)), D((2, 7)), D((2, 7)), D((7,)), D((7,)), D((7,)), D((7,)), D((7,)), D((7,)),
            D((3,)), D((3,)), D((3,)), D((3,)), D((7,)), D((7,)), D((7,)), D((7,)), D(()), D(()),
        ],
        compiler_params=pltpu.CompilerParams(
            collective_id=0, has_side_effects=True, vmem_limit_bytes=60 << 20
        ),
    )(
        act, grad, piece,
        jnp.asarray(gather, BF16), jnp.asarray(perm, BF16), jnp.asarray(spread(), BF16),
    )
    input_grad = jnp.transpose(ig, (1, 0, 2))[None]
    kernel_grad = jnp.transpose(kg, (1, 0, 2))
    return input_grad, kernel_grad


def solution(mesh):
    in_specs = (
        P("band", None, "strip", None),
        P("band", None, "strip", None),
        P("band", None, "strip"),
    )
    out_specs = (P("band", None, "strip", None), P("band", None, "strip"))
    return jax.shard_map(body, mesh=mesh, in_specs=in_specs, out_specs=out_specs, check_vma=False)
```

```python
import math

import jax
import jax.numpy as jnp
import numpy as np
from jax import lax
from jax.experimental import pallas as pl
from jax.experimental.pallas import tpu as pltpu
from jax.sharding import PartitionSpec as P

MESH = pl.DeviceIdType.MESH
BF16 = jnp.bfloat16
F32 = jnp.float32

ROWS = 6
CH = 320
WIDTH = 128
NX, NY, NZ = 4, 8, 8
ZL = 4
KI = 5
KO = 40
HALF = CH // 2
NT = (((1,), (1,)), ((), ()))


def row_order():
    rows = {0: [], 1: [], 2: []}
    for y in range(NY):
        for k in range(4):
            rows[1] += [(zl, y, k) for zl in range(ZL)]
    for zl in range(ZL):
        rows[1] += [(zl, y, 4) for y in range(NY)]
    for ks in ((0, 1), (2, 3, 4)):
        for zl in range(ZL):
            for k in ks:
                rows[0] += [(zl, y, k) for y in range(NY)]
    for zl in range(ZL):
        for k in (0, 1, 2):
            rows[2] += [(zl, y, k) for y in range(NY)]
    for y in range(NY):
        for k in (3, 4):
            rows[2] += [(zl, y, k) for zl in range(ZL)]
    return rows[0] + rows[1] + rows[2]


def permutation():
    perm = np.zeros((CH, CH), np.float32)
    gather = np.zeros((2, 3 * HALF, CH), np.float32)
    for core in range(2):
        for m in range(HALF):
            perm[2 * KI * (m // KI) + KI * core + m % KI, core * HALF + m] = 1.0
        for m, (zl, y, k) in enumerate(row_order()):
            gather[core, m, 2 * KI * (zl * NY + y) + KI * core + k] = 1.0
    return gather, perm


def spread():
    out = np.zeros((3 * HALF, 32 * 16), np.float32)
    for j in range(3):
        for m in range(HALF):
            out[j * HALF + m, 16 * (m // KI) + j * KI + m % KI] = 1.0
    return out


def fdot(a, b, dims=(((1,), (0,)), ((), ()))):
    return lax.dot_general(a, b, dims, preferred_element_type=F32)


def kernel(
    scale, act_hbm, grad_hbm, taps_ref, gather_hbm, permt_hbm, spread_hbm,
    ig_ref, kg_ref,
    piece_ref, act, gext, gather, permt, spr, amat, q, wp, wmat, igs, igr,
    pxe, pxl, pze, pzl, py, rxe, rxl, rze, rzl, ry1,
    sxe, sxl, sz, sy, ry2, rz2, rx2, rx3, ty, tyr, ry3, tz, tzr, rz3,
    lsem, psem, prec, hsem, hrec, fsem, frec, gsem, grec, xsem, xrec, zsem, zrec, y1sem, y1rec,
    y2sem, y2rec, z2sem, z2rec, x2sem, x2rec, x3sem, x3rec, y3sem, y3rec, z3sem, z3rec, isem, irec,
):
    band = lax.axis_index("band")
    strip = lax.axis_index("strip")
    core = lax.rem(band, 2)
    y = lax.rem(band // 2, NY)
    zl = band // (2 * NY)
    x = lax.rem(strip, NX)
    zh = strip // NX
    z = zh * ZL + zl

    def at(zz, yy, xx):
        zzh, zzl = zz // ZL, lax.rem(zz, ZL)
        return ((zzl * NY + yy) * 2 + core, zzh * NX + xx)

    pair = (band + 1 - 2 * core, strip)
    down = (band, lax.rem(strip + 1, 8))
    up = (band, lax.rem(strip + 7, 8))
    xs = [lax.rem(x + d, NX) for d in range(1, NX)]
    ys = [lax.rem(y + d, NY) for d in range(1, NY)]
    zs = [lax.rem(z + d, NZ) for d in range(1, NZ)]
    xdev = [at(z, y, v) for v in xs]
    ydev = [at(z, v, x) for v in ys]
    zdev = [at(v, y, x) for v in zs]

    barrier = pltpu.get_barrier_semaphore()
    partners = [pair, down, up] + xdev + ydev + zdev
    for dev in partners:
        pl.semaphore_signal(barrier, inc=1, device_id=dev, device_id_type=MESH)

    local = [
        pltpu.make_async_copy(grad_hbm, gext.at[0, pl.ds(1, ROWS)], lsem.at[1]),
        pltpu.make_async_copy(act_hbm, act.at[0], lsem.at[0]),
        pltpu.make_async_copy(gather_hbm.at[core], gather, lsem.at[2]),
        pltpu.make_async_copy(permt_hbm, permt, lsem.at[3]),
        pltpu.make_async_copy(spread_hbm, spr, lsem.at[4]),
    ]
    for c in local:
        c.start()
    rows = []
    for j in range(3):
        cols = [taps_ref[3 * j + c].astype(F32) for c in range(3)]
        rows.append(jnp.concatenate(cols + [jnp.zeros((KI, 8), F32)], axis=1))
    block = jnp.concatenate(rows + [jnp.zeros((1, 128), F32)], axis=0).reshape(2, 8, 128)
    piece_ref[...] = block.astype(BF16)
    wp[:, zh, x, zl, y] = block.astype(BF16)
    tyr[...] = jnp.zeros_like(tyr)
    tzr[...] = jnp.zeros_like(tzr)

    sent = []

    def remote(src, dst, ss, rs, dev):
        c = pltpu.make_async_remote_copy(
            src_ref=src, dst_ref=dst, send_sem=ss, recv_sem=rs, device_id=dev, device_id_type=MESH
        )
        c.start()
        sent.append(c)
        return c

    def received(copies):
        for c in copies:
            c.wait_recv()

    pl.semaphore_wait(barrier, len(partners))
    inner, outer = strip > 0, strip < 7
    halo_down = []
    halo_up = []
    for n in range(4):
        part = pl.ds(80 * n, 80)
        halo_down.append(
            pltpu.make_async_remote_copy(
                src_ref=grad_hbm.at[ROWS - 1, part], dst_ref=gext.at[0, 0, part],
                send_sem=hsem.at[0, n], recv_sem=hrec.at[0, n], device_id=down, device_id_type=MESH,
            )
        )
        halo_up.append(
            pltpu.make_async_remote_copy(
                src_ref=grad_hbm.at[0, part], dst_ref=gext.at[0, ROWS + 1, part],
                send_sem=hsem.at[1, n], recv_sem=hrec.at[1, n], device_id=up, device_id_type=MESH,
            )
        )

    @pl.when(outer)
    def _():
        for c in halo_down:
            c.start()

    @pl.when(inner)
    def _():
        for c in halo_up:
            c.start()

    here = (zh, x, zl, y)
    gx = [
        remote(piece_ref.at[1], wp.at[(1, *here)], gsem.at[i], grec.at[i], xdev[i])
        for i in (1, 0, 2)
    ]
    gy = [
        remote(piece_ref.at[0], wp.at[(0, *here)], gsem.at[3 + i], grec.at[3 + i], ydev[i])
        for i in (3, 2, 4, 1, 5, 0, 6)
    ]
    swap = [
        remote(grad_hbm, gext.at[1, pl.ds(1, ROWS)], psem.at[0], prec.at[0], pair),
        remote(act_hbm, act.at[1], psem.at[1], prec.at[1], pair),
    ]

    lane = lax.broadcasted_iota(jnp.int32, (80, WIDTH), 1)
    zero8 = jnp.zeros((8, WIDTH), F32)

    def fill(img, e, keep=None, parts=range(4)):
        col = pl.ds(pl.multiple_of((img * 8 + e) * WIDTH, WIDTH), WIDTH)
        for pr in parts:
            g = gext[img, e, 80 * pr : 80 * pr + 80, :].astype(F32)
            if keep is not None:
                g = jnp.where(keep, g, 0.0)
            nxt = jnp.where(lane == WIDTH - 1, 0.0, pltpu.roll(g, WIDTH - 1, 1))
            prv = jnp.where(lane == 0, 0.0, pltpu.roll(g, 1, 1))
            for h in range(2):
                sl = slice(40 * h, 40 * h + 40)
                block = jnp.concatenate([nxt[sl], g[sl], prv[sl], zero8], axis=0)
                base = (2 * pr + h) * 128
                q[base : base + 128, col] = block.astype(BF16)

    def fill_image(img):
        @pl.loop(1, ROWS + 1)
        def _(e):
            fill(img, e)

    def rows_image(img):
        for h in range(0, ROWS, 2):
            both = jnp.concatenate([act[img, h], act[img, h + 1]], axis=1)
            base = img * ROWS * WIDTH + h * WIDTH
            amat[:, base : base + 2 * WIDTH] = fdot(gather[...], both).astype(BF16)

    def forward(n):
        part = pl.ds(80 * n, 80)

        @pl.when(inner)
        def _():
            halo_down[n].wait_recv()

        @pl.when(outer)
        def _():
            halo_up[n].wait_recv()

        return [
            remote(gext.at[0, e, part], gext.at[1, e, part], fsem.at[i, n], frec.at[i, n], pair)
            for i, e in enumerate((0, ROWS + 1))
        ]

    local[0].wait()
    fill_image(0)
    local[1].wait()
    local[2].wait()
    rows_image(0)
    swap[0].wait_recv()
    fill_image(1)
    swap[1].wait_recv()
    rows_image(1)
    span = ROWS * WIDTH

    def product(j, n):
        rows = pl.ds(256 * n if isinstance(n, int) else pl.multiple_of(n * 256, 256), 256)
        mine = slice(HALF * j, HALF * j + HALF)
        total = fdot(amat[mine, 0:span], q[rows, (2 - j) * WIDTH : (2 - j) * WIDTH + span], NT)
        return total + fdot(
            amat[mine, span : 2 * span], q[rows, (10 - j) * WIDTH : (10 - j) * WIDTH + span], NT
        )

    @pl.loop(0, 4)
    def _(n):
        total = product(1, n)
        for h in range(2):
            sh, sx = n // 2, 2 * lax.rem(n, 2) + h
            one = total[:, 128 * h : 128 * h + 128]
            pxe[sh, sx] = one[:128].reshape(NY, 16, 128)
            pze[sh, sx] = one[128:].reshape(ZL, 8, 128)

    xe = [
        remote(pxe.at[:, xs[i]], rxe.at[i], xsem.at[0, i], xrec.at[0, i], xdev[i]) for i in (1, 0, 2)
    ]
    ze = [
        remote(
            pze.at[zs[i] // ZL, :, lax.rem(zs[i], ZL)], rze.at[i], zsem.at[0, i], zrec.at[0, i], zdev[i]
        )
        for i in (3, 2, 4, 1, 5, 0, 6)
    ]

    received(gx)
    gz1 = [
        remote(wp.at[1, zh, :, zl, y], wp.at[1, zh, :, zl, y], gsem.at[10 + i], grec.at[10 + i], zdev[i])
        for i in (3, 2, 4, 1, 5, 0, 6)
    ]
    received(gy)
    gz0 = [
        remote(wp.at[0, zh, x, zl], wp.at[0, zh, x, zl], gsem.at[17 + i], grec.at[17 + i], zdev[i])
        for i in (3, 2, 4, 1, 5, 0, 6)
    ]
    ahead = forward(0)
    for n in range(4):
        now = ahead
        if n < 3:
            ahead = forward(n + 1)
        fill(0, 0, inner, (n,))
        fill(0, ROWS + 1, outer, (n,))
        now[0].wait_recv()
        fill(1, 0, inner, (n,))
        now[1].wait_recv()
        fill(1, ROWS + 1, outer, (n,))
        first = product(0, n)
        third = product(2, n)
        for h in range(2):
            sh, sx = n // 2, 2 * (n % 2) + h
            one = first[:, 128 * h : 128 * h + 128]
            pxl[sh, sx, :, 0:16] = one[:64].reshape(ZL, 16, 128)
            pzl[sh, sx] = one[64:].reshape(ZL, 24, 128)
            one = third[:, 128 * h : 128 * h + 128]
            pxl[sh, sx, :, 16:40] = one[:96].reshape(ZL, 24, 128)
            py[sh, sx] = one[96:].reshape(NY, 8, 128)

    zlate = [
        remote(
            pzl.at[zs[i] // ZL, :, lax.rem(zs[i], ZL)], rzl.at[i], zsem.at[1, i], zrec.at[1, i], zdev[i]
        )
        for i in (3, 2, 4, 1, 5, 0, 6)
    ]
    y1 = [remote(py.at[:, :, ys[i]], ry1.at[i], y1sem.at[i], y1rec.at[i], ydev[i]) for i in (3, 2, 4, 1, 5, 0, 6)]
    xl = [
        remote(pxl.at[:, xs[i]], rxl.at[i], xsem.at[1, i], xrec.at[1, i], xdev[i]) for i in (1, 0, 2)
    ]

    received(gz1)
    gy1 = [
        remote(wp.at[1, :, :, :, y], wp.at[1, :, :, :, y], gsem.at[24 + i], grec.at[24 + i], ydev[i])
        for i in (3, 2, 4, 1, 5, 0, 6)
    ]
    received(gz0)
    gx0 = [
        remote(wp.at[0, :, x], wp.at[0, :, x], gsem.at[31 + i], grec.at[31 + i], xdev[i])
        for i in (1, 0, 2)
    ]
    received(xe)
    for h in range(2):
        total = pxe[h, x]
        for i in range(3):
            total = total + rxe[i, h]
        sxe[h] = total
    y2 = [remote(sxe.at[:, ys[i]], ry2.at[i], y2sem.at[i], y2rec.at[i], ydev[i]) for i in (3, 2, 4, 1, 5, 0, 6)]
    received(y1)
    total = py[:, :, y]
    for i in range(7):
        total = total + ry1[i]
    sy[...] = total
    x3 = [remote(sy.at[:, xs[i]], rx3.at[i], x3sem.at[i], x3rec.at[i], xdev[i]) for i in (1, 0, 2)]
    received(xl)
    for h in range(2):
        total = pxl[h, x]
        for i in range(3):
            total = total + rxl[i, h]
        sxl[h] = total
    z2 = [
        remote(sxl.at[zs[i] // ZL, lax.rem(zs[i], ZL)], rz2.at[i], z2sem.at[i], z2rec.at[i], zdev[i])
        for i in (3, 2, 4, 1, 5, 0, 6)
    ]
    received(ze)
    received(zlate)
    early = pze[zh, :, zl]
    late = pzl[zh, :, zl]
    for i in range(7):
        early = early + rze[i]
        late = late + rzl[i]
    sz[:, 0:8] = early
    sz[:, 8:32] = late
    x2 = [remote(sz.at[xs[i]], rx2.at[i], x2sem.at[i], x2rec.at[i], xdev[i]) for i in (1, 0, 2)]

    received(y2)
    total = sxe[:, y]
    for i in range(7):
        total = total + ry2[i]
    tz[:, 0:16] = total
    received(x3)
    total = sy[:, x]
    for i in range(3):
        total = total + rx3[i]
    tz[:, 16:24] = total
    for h in range(2):
        for v in range(ZL):
            for k in range(6):
                tzr[h, v, k : k + 1, :] = tz[h, ZL * k + v : ZL * k + v + 1, :]
    z3 = [
        remote(tzr.at[zs[i] // ZL, lax.rem(zs[i], ZL)], rz3.at[i], z3sem.at[i], z3rec.at[i], zdev[i])
        for i in (3, 2, 4, 1, 5, 0, 6)
    ]
    received(z2)
    total = sxl[zh, zl]
    for i in range(7):
        total = total + rz2[i]
    ty[0:40] = total
    received(x2)
    total = sz[x]
    for i in range(3):
        total = total + rx2[i]
    ty[40:72] = total
    for v in range(NY):
        for k in range(9):
            tyr[v, k : k + 1, :] = ty[NY * k + v : NY * k + v + 1, :]
    y3 = [remote(tyr.at[ys[i]], ry3.at[i], y3sem.at[i], y3rec.at[i], ydev[i]) for i in (3, 2, 4, 1, 5, 0, 6)]

    received(gx0)
    received(gy1)
    local[4].wait()
    for pr in range(4):
        cols = []
        for sidx in (2 * pr, 2 * pr + 1):
            halves = [
                wp[half, sidx // NX, sidx % NX].astype(F32).reshape(32, 8, 128) for half in range(2)
            ]
            cols.append(jnp.concatenate(halves, axis=1).reshape(512, 128).astype(BF16))
        both = jnp.concatenate(cols, axis=1)
        wmat[:, 256 * pr : 256 * pr + 256] = fdot(spr[...], both).astype(BF16)

    def image(img, put):
        for h in range(0, ROWS, 2):
            total = None
            for j in range(3):
                base = (img * 8 + h + 2 - j) * WIDTH
                term = fdot(wmat[HALF * j : HALF * j + HALF, :], q[:, base : base + 256])
                total = term if total is None else total + term
            total = total.astype(BF16)
            put(h, total[:, :WIDTH])
            put(h + 1, total[:, WIDTH:])

    mine = pl.ds(pl.multiple_of(core * HALF, HALF), HALF)

    def put_peer(h, v):
        igs[h] = v

    def put_own(h, v):
        igr[h, mine, :] = v

    image(1, put_peer)
    back = remote(igs, igr.at[:, mine], isem, irec, pair)

    image(0, put_own)
    local[3].wait()
    back.wait_recv()
    for h in range(0, ROWS, 2):
        both = jnp.concatenate([igr[h], igr[h + 1]], axis=1)
        out = fdot(permt[...], both).astype(BF16)
        ig_ref[h] = out[:, :WIDTH]
        ig_ref[h + 1] = out[:, WIDTH:]

    received(z3)
    total = tzr[zh, zl]
    for i in range(7):
        total = total + rz3[i]
    total = total * scale

    def put(j, k0, rows):
        for c in range(3):
            kg_ref[3 * j + c, k0 : k0 + rows.shape[0], :] = rows[:, 40 * c : 40 * c + 40]

    put(1, 0, total[0:4])
    put(2, 3, total[4:6])
    received(y3)
    total = tyr[y]
    for i in range(7):
        total = total + ry3[i]
    total = total * scale
    put(0, 0, total[0:2])
    put(2, 0, total[2:5])
    put(1, 4, total[5:6])
    put(0, 2, total[6:9])
    for c in sent:
        c.wait_send()

    @pl.when(outer)
    def _():
        for c in halo_down:
            c.wait_send()

    @pl.when(inner)
    def _():
        for c in halo_up:
            c.wait_send()


def body(activations, out_grad, weights):
    cells = 64 * 48 * 128
    scale = 1.0 / math.sqrt(cells)
    act = jnp.transpose(activations[0], (1, 0, 2))
    grad = jnp.transpose(out_grad[0], (1, 0, 2))
    piece = jnp.transpose(weights, (1, 0, 2))
    gather, perm = permutation()
    hbm = pl.BlockSpec(memory_space=pltpu.HBM)
    vmem = pl.BlockSpec(memory_space=pltpu.VMEM)
    V = pltpu.VMEM
    D = pltpu.SemaphoreType.DMA

    def run(*args):
        kernel(scale, *args)

    ig, kg = pl.pallas_call(
        run,
        out_shape=(
            jax.ShapeDtypeStruct((ROWS, CH, WIDTH), BF16),
            jax.ShapeDtypeStruct((9, KI, KO), F32),
        ),
        in_specs=[hbm, hbm, vmem, hbm, hbm, hbm],
        out_specs=(vmem, vmem),
        scratch_shapes=[
            V((2, 8, 128), BF16),
            V((2, ROWS, CH, WIDTH), BF16),
            V((2, 8, CH, WIDTH), BF16),
            V((3 * HALF, CH), BF16),
            V((CH, CH), BF16),
            V((3 * HALF, 512), BF16),
            V((3 * HALF, 2 * ROWS * WIDTH), BF16),
            V((1024, 2048), BF16),
            V((2, 2, NX, ZL, NY, 8, 128), BF16),
            V((3 * HALF, 1024), BF16),
            V((ROWS, HALF, WIDTH), BF16),
            V((ROWS, CH, WIDTH), BF16),
            V((2, NX, NY, 16, 128), F32),
            V((2, NX, ZL, 40, 128), F32),
            V((2, NX, ZL, 8, 128), F32),
            V((2, NX, ZL, 24, 128), F32),
            V((2, NX, NY, 8, 128), F32),
            V((3, 2, NY, 16, 128), F32),
            V((3, 2, ZL, 40, 128), F32),
            V((7, NX, 8, 128), F32),
            V((7, NX, 24, 128), F32),
            V((7, 2, NX, 8, 128), F32),
            V((2, NY, 16, 128), F32),
            V((2, ZL, 40, 128), F32),
            V((NX, 32, 128), F32),
            V((2, NX, 8, 128), F32),
            V((7, 2, 16, 128), F32),
            V((7, 40, 128), F32),
            V((3, 32, 128), F32),
            V((3, 2, 8, 128), F32),
            V((72, 128), F32),
            V((NY, 16, 128), F32),
            V((7, 16, 128), F32),
            V((2, 24, 128), F32),
            V((2, ZL, 8, 128), F32),
            V((7, 8, 128), F32),
            D((5,)), D((2,)), D((2,)), D((2, 4)), D((2, 4)), D((2, 4)), D((2, 4)), D((34,)), D((34,)),
            D((2, 3)), D((2, 3)), D((2, 7)), D((2, 7)), D((7,)), D((7,)), D((7,)), D((7,)), D((7,)), D((7,)),
            D((3,)), D((3,)), D((3,)), D((3,)), D((7,)), D((7,)), D((7,)), D((7,)), D(()), D(()),
        ],
        compiler_params=pltpu.CompilerParams(
            collective_id=0, has_side_effects=True, vmem_limit_bytes=60 << 20
        ),
    )(
        act, grad, piece,
        jnp.asarray(gather, BF16), jnp.asarray(perm, BF16), jnp.asarray(spread(), BF16),
    )
    input_grad = jnp.transpose(ig, (1, 0, 2))[None]
    kernel_grad = jnp.transpose(kg, (1, 0, 2))
    return input_grad, kernel_grad


def solution(mesh):
    in_specs = (
        P("band", None, "strip", None),
        P("band", None, "strip", None),
        P("band", None, "strip"),
    )
    out_specs = (P("band", None, "strip", None), P("band", None, "strip"))
    return jax.shard_map(body, mesh=mesh, in_specs=in_specs, out_specs=out_specs, check_vma=False)
```
